1024 devices in a mesh: ctx: 32 (over z, core), grp: 32 (over y, x).
Axes of the slice: x: 4, y: 8, z: 16, core: 2. Of those that a mesh axis runs over, the one named last changes fastest.
Arguments:
- queries: bfloat16 [1, 131072, 4096], P(None, ('ctx', 'grp')), may hold values from -200 to 200
- keyvals: bfloat16 [2, 1, 131072, 512], P(None, None, ('ctx', 'grp')), may hold values from -8 to 8
- seg_len: int32 [1, 512], replicated, may hold values from 128 to 384, as said below
- seg_task: int32 [1, 512], replicated, may hold values from 0 to 191
- task_slot: int32 [192], replicated, may hold values from 0 to 191, each once
- prefix_bank: bfloat16 [2, 192, 16, 512], P(None, 'grp'), may hold values from -9 to 9
Outputs:
- attended: bfloat16 [1, 131072, 4096], P(None, ('ctx', 'grp'))
The draws below stay inside these ranges and needn't reach their ends.
Inputs may be any that keep to these rules, and one draw needn't show every extreme that they name: `seg_len`: the 512 lengths sum to 131072, and at least one equals 384. `task_slot`: A permutation; bank row r is held by index r // 6 of grp.
All inputs are finite; a program needn't handle non-finite values.
Results may differ from the reference program's by a relative error of at most 0.004.
Values may be sent and summed in bfloat16 or wider, within the bound.
A program may use at most 32 MiB of HBM per device.

```python
import math
import jax
import jax.numpy as jnp
from jax import lax

H = 32
KVH = 4
HD = 128
T_DEV = 128
PREFIX = 16
HOPS = 3
ROWS = 1
ROW_LEN = 131072
MOST = 384
SEGS = 512
TASKS = 192


def joint_draw(key):
    base = jax.random.fold_in(key, 11)
    key_q, key_k, key_v = jax.random.split(base, 3)
    groups = H // KVH
    keys_all = jnp.clip(jax.random.normal(key_k, (ROWS, ROW_LEN, KVH, HD), jnp.float32), -6.0, 6.0)
    values_all = jnp.clip(jax.random.normal(key_v, (ROWS, ROW_LEN, KVH, HD), jnp.float32), -6.0, 6.0)
    queries_all = jnp.clip(jax.random.normal(key_q, (ROWS, ROW_LEN, KVH, groups, HD), jnp.float32), -6.0, 6.0)
    return (queries_all, keys_all, values_all)


def draw_queries(key, part):
    queries_all, keys_all, values_all = joint_draw(key)
    return queries_all.reshape(ROWS, ROW_LEN, H * HD).astype(jnp.bfloat16)


def draw_keyvals(key, part):
    queries_all, keys_all, values_all = joint_draw(key)
    stacked = jnp.stack([keys_all.reshape(ROWS, ROW_LEN, KVH * HD), values_all.reshape(ROWS, ROW_LEN, KVH * HD)])
    return stacked.astype(jnp.bfloat16)


def draw_seg_len(key, part):
    key_split, key_order = jax.random.split(jax.random.fold_in(key, 23))
    pair_count = (ROW_LEN // T_DEV - HOPS) // (HOPS + 1)
    moved = jax.random.randint(key_split, (ROWS, pair_count), 0, (HOPS - 1) * T_DEV + 1)
    first_part = T_DEV + moved
    second_part = HOPS * T_DEV - moved
    paired = jnp.stack([first_part, second_part], axis=2).reshape(ROWS, 2 * pair_count)
    listed = jnp.concatenate([paired, jnp.full((ROWS, 1), T_DEV, jnp.int32), jnp.full((ROWS, 1), MOST, jnp.int32)], axis=1).astype(jnp.int32)
    orders = jax.vmap(lambda sub_key: jax.random.permutation(sub_key, SEGS))(jax.random.split(key_order, ROWS))
    return jnp.take_along_axis(listed, orders.astype(jnp.int32), axis=1).astype(jnp.int32)


def with_ends(entries, own_key, low, top_value):
    spot = [jax.random.randint(jax.random.fold_in(own_key, axis), (), 0, length) for axis, length in enumerate(entries.shape)]
    main_axis = entries.shape.index(max(entries.shape))
    neighbour = spot[:main_axis] + [(spot[main_axis] + 1) % entries.shape[main_axis]] + spot[main_axis + 1:]
    return entries.at[tuple(spot)].set(low).at[tuple(neighbour)].set(top_value)


def levels(stream_key, extent, pieces, low, largest):
    loudness = 1.0
    for axis_at, shards_of in pieces:
        heights = jax.random.uniform(jax.random.fold_in(jax.random.fold_in(stream_key, 6), axis_at), (shards_of,), jnp.float32, low / len(pieces), largest / len(pieces))
        loudness = loudness * jnp.repeat(jnp.exp(heights), extent[axis_at] // shards_of).reshape((-1,) + (1,) * (len(extent) - 1 - axis_at))
    return loudness


def normal_values(own_key, shape, scale, bound, shards=(), kind=jnp.bfloat16):
    loudness = levels(own_key, shape, shards, -0.22, 0.18) if shards else 1.0
    array = jax.random.normal(own_key, shape, jnp.float32) * scale * loudness
    return jnp.minimum(jnp.maximum(array, -bound), bound).astype(kind)


def setup_inputs(seed: int = 0) -> dict:
    streams_of = jax.random.split(jax.random.key(seed), 7)
    return {
        "queries": draw_queries(jax.random.fold_in(streams_of[6], 71), 0),
        "keyvals": draw_keyvals(jax.random.fold_in(streams_of[6], 71), 0),
        "seg_len": draw_seg_len(jax.random.fold_in(streams_of[6], 71), 0),
        "seg_task": with_ends(jax.random.randint(streams_of[3], (ROWS, SEGS), 0, TASKS), jax.random.fold_in(streams_of[3], 1), 0, TASKS - 1).astype(jnp.int32),
        "task_slot": jax.random.permutation(streams_of[4], TASKS).astype(jnp.int32),
        "prefix_bank": normal_values(streams_of[5], (2, TASKS, PREFIX, KVH * HD), 1.5, 9.0, ((1, 32),)),
    }


def segment_index(starts, positions):
    return lax.optimization_barrier(jnp.sum((starts[None, :] <= positions[:, None]).astype(jnp.int32), axis=1)) - 1

def reference(queries, keyvals, seg_len, seg_task, task_slot, prefix_bank):
    groups = H // KVH
    score_scale = 1.0 / math.sqrt(HD)
    window_len = MOST + T_DEV

    def one_row(row_index):
        row_q = queries[row_index]
        row_kv = keyvals[:, row_index]
        lengths = seg_len[row_index]
        row_tasks = seg_task[row_index]
        starts = jnp.cumsum(lengths) - lengths
        padded = jnp.concatenate([jnp.zeros((2, MOST, KVH * HD), keyvals.dtype), row_kv], axis=1)

        def one_block(block_index):
            first = block_index * T_DEV
            block_q = lax.dynamic_slice_in_dim(row_q, first, T_DEV, 0).reshape(T_DEV, KVH, groups, HD).astype(jnp.float32)
            window = lax.dynamic_slice_in_dim(padded, first, window_len, 1).reshape(2, window_len, KVH, HD).astype(jnp.float32)
            query_pos = first + jnp.arange(T_DEV, dtype=jnp.int32)
            key_pos = first - MOST + jnp.arange(window_len, dtype=jnp.int32)
            query_seg = segment_index(starts, query_pos)
            key_seg = segment_index(starts, key_pos)
            allowed = (key_seg[None, :] == query_seg[:, None]) & (key_pos[None, :] <= query_pos[:, None])
            query_task = row_tasks[query_seg]
            bank_row = task_slot[query_task]
            prefix = prefix_bank[:, bank_row].reshape(2, T_DEV, PREFIX, KVH, HD).astype(jnp.float32)
            local_scores = jnp.einsum('tkgd,skd->kgts', block_q, window[0]) * score_scale
            prefix_scores = jnp.einsum('tkgd,tpkd->kgtp', block_q, prefix[0]) * score_scale
            scores = jnp.concatenate([local_scores, prefix_scores], axis=-1)
            mask_full = jnp.concatenate([jnp.broadcast_to(allowed, (KVH, groups, T_DEV, window_len)), jnp.ones((KVH, groups, T_DEV, PREFIX), dtype=bool)], axis=-1)
            top_score = lax.optimization_barrier(jnp.max(jnp.where(mask_full, scores, -jnp.inf), axis=-1, keepdims=True))
            weights = jnp.where(mask_full, jnp.exp(scores - top_score), 0.0)
            total = lax.optimization_barrier(jnp.sum(weights, axis=-1))
            rounded = lax.optimization_barrier(weights.astype(jnp.bfloat16)).astype(jnp.float32)
            mixed = jnp.einsum('kgts,skd->kgtd', rounded[..., :window_len], window[1])
            mixed = mixed + jnp.einsum('kgtp,tpkd->kgtd', rounded[..., window_len:], prefix[1])
            result = mixed / total[..., None]
            return result.transpose(2, 0, 1, 3).reshape(T_DEV, H * HD).astype(jnp.bfloat16)
        blocks = lax.map(one_block, jnp.arange(ROW_LEN // T_DEV, dtype=jnp.int32))
        return blocks.reshape(ROW_LEN, H * HD)
    return lax.map(one_row, jnp.arange(ROWS, dtype=jnp.int32))
```

```python
import math

import jax
import jax.numpy as jnp
from jax import lax
from jax.experimental import pallas as pl
from jax.experimental.pallas import tpu as pltpu
from jax.sharding import PartitionSpec as P

H = 32
KVH = 4
HD = 128
GROUPS = H // KVH
T = 128
PREFIX = 16
SEGS = 512
ROWS6 = 6
HALF = ROWS6 // 2
NX = 4
NY = 8
KEYS = 4 * T
SLOTS = KEYS + 2 * PREFIX
EXP_SCALE = math.log2(math.e) / math.sqrt(HD)
NEG = -1e30
BIG = 1 << 30


def scan_lanes(row):
    lane = lax.broadcasted_iota(jnp.int32, row.shape, 1)
    step = 1
    while step < row.shape[1]:
        row = row + jnp.where(lane >= step, pltpu.roll(row, step, 1), 0)
        step *= 2
    return row


def kernel(
    q_hbm,
    kv_hbm,
    len_hbm,
    task_hbm,
    slot_smem,
    bank_hbm,
    out_hbm,
    q_buf,
    kv_buf,
    pass_buf,
    col_bank,
    pick_out,
    pick_in,
    acc_buf,
    max_buf,
    bias_buf,
    pbias_buf,
    out_buf,
    len_buf,
    task_buf,
    local_sem,
    out_sem,
    kv_send,
    kv_recv,
    ring_send,
    ring_recv,
    sib_send,
    sib_recv,
    pick_send,
    pick_recv,
):
    ctx = lax.axis_index("ctx")
    grp = lax.axis_index("grp")
    n_ctx = lax.axis_size("ctx")
    core = ctx % 2
    x = grp % NX
    y = grp // NX
    shard = ctx * (NX * NY) + grp

    next_ctx = jnp.where(y == NY - 1, (ctx + 1) % n_ctx, ctx)
    prev_ctx = jnp.where(y == 0, (ctx + n_ctx - 1) % n_ctx, ctx)
    up = (y + 1) % NY
    down = (y + NY - 1) % NY

    def in_row(col):
        return {"ctx": ctx, "grp": y * NX + col}

    def in_next(col):
        return {"ctx": next_ctx, "grp": up * NX + col}

    def in_prev(col):
        return {"ctx": prev_ctx, "grp": down * NX + col}

    ring_up = {"ctx": ctx, "grp": up * NX + x}
    ring_down = {"ctx": ctx, "grp": down * NX + x}
    sibling = {"ctx": ctx + 1 - 2 * core, "grp": grp}

    kv_local = []
    for j in range(KVH):
        copy = pltpu.make_async_copy(
            kv_hbm.at[:, 0, :, pl.ds(j * HD, HD)],
            kv_buf.at[j, :, pl.ds(0, T), :],
            local_sem.at[j],
        )
        copy.start()
        kv_local.append(copy)
    bank_local = pltpu.make_async_copy(bank_hbm, col_bank.at[y], local_sem.at[4])
    bank_local.start()
    len_copy = pltpu.make_async_copy(len_hbm, len_buf, local_sem.at[5])
    len_copy.start()
    task_copy = pltpu.make_async_copy(task_hbm, task_buf, local_sem.at[6])
    task_copy.start()
    q_copy = pltpu.make_async_copy(q_hbm.at[0], q_buf, local_sem.at[7])
    q_copy.start()

    barrier = pltpu.get_barrier_semaphore()

    def greet(device):
        pl.semaphore_signal(barrier, inc=1, device_id=device, device_id_type=pl.DeviceIdType.MESH)

    for hop in range(1, NX):
        greet(in_row((x + hop) % NX))
    greet(ring_up)
    greet(ring_down)
    greet(sibling)

    @pl.when(y == NY - 1)
    def _():
        greet(in_next(x))

    @pl.when(y == 0)
    def _():
        greet(in_prev(x))

    @pl.when(x == 0)
    def _():
        greet(in_prev(NX - 1))

    @pl.when(x == NX - 1)
    def _():
        greet(in_next(0))

    edge_y = jnp.where((y == 0) | (y == NY - 1), 1, 0)
    edge_x = jnp.where((x == 0) | (x == NX - 1), 1, 0)
    pl.semaphore_wait(barrier, 6 + edge_y + edge_x)

    def slot_ref(j, slot):
        if slot == 4:
            return pass_buf.at[j]
        return kv_buf.at[j, :, pl.ds(slot * T, T), :]

    def kv_copy(j, number, source, device, target):
        return pltpu.make_async_remote_copy(
            src_ref=slot_ref(j, source),
            dst_ref=slot_ref(j, target),
            send_sem=kv_send.at[number, j],
            recv_sem=kv_recv.at[target - 1, j],
            device_id=device,
            device_id_type=pl.DeviceIdType.MESH,
        )

    def wait_kv(j, slot):
        kv_copy(j, 0, slot, sibling, slot).wait_recv()

    def ring_copy(number, owner, device):
        piece = col_bank.at[owner, :, pl.ds(HALF * core, HALF)]
        return pltpu.make_async_remote_copy(
            src_ref=piece,
            dst_ref=piece,
            send_sem=ring_send.at[number],
            recv_sem=ring_recv.at[number],
            device_id=device,
            device_id_type=pl.DeviceIdType.MESH,
        )

    def sib_copy(number, owner, half):
        piece = col_bank.at[owner, :, pl.ds(HALF * half, HALF)]
        return pltpu.make_async_remote_copy(
            src_ref=piece,
            dst_ref=piece,
            send_sem=sib_send.at[number],
            recv_sem=sib_recv.at[number],
            device_id=sibling,
            device_id_type=pl.DeviceIdType.MESH,
        )

    def down_copy(step):
        return ring_copy(step, (y + step) % NY, ring_down)

    def up_copy(step):
        return ring_copy(4 + step, (y + NY - step) % NY, ring_up)

    bank_local.wait()
    down_copy(0).start()
    up_copy(0).start()
    for j in range(KVH):
        kv_local[j].wait()

        @pl.when(x < NX - 1)
        def _():
            kv_copy(j, 0, 0, in_row((x + 1) % NX), 1).start()

        @pl.when(x > 0)
        def _():
            kv_copy(j, 1, 0, in_next(x), 4).start()

        @pl.when(x == 0)
        def _():
            kv_copy(j, 1, 0, in_row(NX - 1), 3).start()

    len_copy.wait()
    task_copy.wait()
    lengths = len_buf[...]
    starts = scan_lanes(lengths) - lengths
    tasks = task_buf[...]

    def segments(first):
        start_a = jnp.max(jnp.where(starts <= first, starts, 0))
        start_b = jnp.min(jnp.where(starts > first, starts, BIG))
        return start_a, start_b

    def bank_row(start):
        task = jnp.sum(jnp.where(starts == start, tasks, 0))
        row = slot_smem[task]
        owner = (row * 10923) >> 16
        return owner % NX, owner // NX, row - ROWS6 * owner

    here_a, here_b = segments(shard * T)
    rel_a = here_a - shard * T
    rel_b = here_b - shard * T

    query_at = lax.broadcasted_iota(jnp.int32, (T, KEYS), 0)
    column = lax.broadcasted_iota(jnp.int32, (T, KEYS), 1)
    key_at = (column % T) - (column // T) * T
    earliest = jnp.where(query_at < rel_b, rel_a, rel_b)
    bias_buf[...] = jnp.where((key_at >= earliest) & (key_at <= query_at), 0.0, NEG)
    query_at = lax.broadcasted_iota(jnp.int32, (T, 2 * PREFIX), 0)
    column = lax.broadcasted_iota(jnp.int32, (T, 2 * PREFIX), 1)
    pbias_buf[...] = jnp.where((query_at < rel_b) == (column < PREFIX), 0.0, NEG)

    q_copy.wait()
    ones = jnp.ones((KEYS, HD), jnp.bfloat16)
    row_parity = core
    next_parity = next_ctx % 2
    prev_parity = prev_ctx % 2

    def relay(j):
        @pl.when(x > 0)
        def _():
            wait_kv(j, 4)

        @pl.when((x == 1) | (x == 2))
        def _():
            kv_copy(j, 2, 4, in_row(x - 1), 3).start()

        @pl.when(x == 3)
        def _():
            kv_copy(j, 2, 4, in_row(2), 3).start()
            kv_copy(j, 3, 4, in_row(0), 1).start()

        wait_kv(j, 1)

        @pl.when((row_parity == 0) & ((x == 1) | (x == 2)))
        def _():
            kv_copy(j, 3, 1, in_row(x + 1), 2).start()

        @pl.when((row_parity == 1) & (x == 0))
        def _():
            kv_copy(j, 2, 1, in_row(1), 2).start()

        @pl.when((x == 3) & (next_parity == 1))
        def _():
            kv_copy(j, 4, 1, in_next(0), 2).start()

        wait_kv(j, 3)

        @pl.when((row_parity == 0) & ((x == 1) | (x == 2)))
        def _():
            kv_copy(j, 4, 3, in_row(x - 1), 2).start()

        @pl.when((row_parity == 1) & (x == 3))
        def _():
            kv_copy(j, 5, 3, in_row(2), 2).start()

        @pl.when((x == 0) & (prev_parity == 1))
        def _():
            kv_copy(j, 3, 3, in_prev(NX - 1), 2).start()

        wait_kv(j, 2)

    def row_keys(j):
        keys = kv_buf[j, 0, pl.ds(0, KEYS), :]
        values = jnp.concatenate([kv_buf[j, 1, pl.ds(0, KEYS), :], ones], axis=1)
        for g in range(GROUPS):
            query = q_buf[:, pl.ds(pl.multiple_of((j * GROUPS + g) * HD, HD), HD)]
            scores = lax.dot_general(
                query, keys, (((1,), (1,)), ((), ())), preferred_element_type=jnp.float32
            )
            scores = scores + bias_buf[...]
            top = jnp.max(scores, axis=1, keepdims=True)
            weights = jnp.exp2((scores - top) * EXP_SCALE).astype(jnp.bfloat16)
            acc_buf[j, g] = jnp.dot(weights, values, preferred_element_type=jnp.float32)
            max_buf[j, g] = jnp.broadcast_to(top, (T, HD))

    def ring_step(step):
        ring_copy(step, (y + 1 + step) % NY, ring_down).wait_recv()
        if step < 3:
            down_copy(step + 1).start()
        sib_copy(step, (y + 1 + step) % NY, core).start()
        if step < 3:
            ring_copy(4 + step, (y + NY - 1 - step) % NY, ring_up).wait_recv()
            if step < 2:
                up_copy(step + 1).start()
            sib_copy(4 + step, (y + NY - 1 - step) % NY, core).start()

    for j in range(KVH):
        ring_step(j)
        relay(j)
        row_keys(j)

    for step in range(4):
        sib_copy(step, (y + 1 + step) % NY, 1 - core).wait_recv()
    for step in range(3):
        sib_copy(4 + step, (y + NY - 1 - step) % NY, 1 - core).wait_recv()

    def pick(col):
        first = (shard - x + col) * T
        start_a, start_b = segments(first)
        rows = []
        for start in (start_a, start_b):
            _, owner_y, row = bank_row(start)
            rows.append(col_bank[owner_y, :, row])
        return rows

    def pick_copy(hop, col):
        return pltpu.make_async_remote_copy(
            src_ref=pick_out.at[hop - 1],
            dst_ref=pick_in.at[hop],
            send_sem=pick_send.at[hop - 1],
            recv_sem=pick_recv.at[hop - 1],
            device_id=in_row(col),
            device_id_type=pl.DeviceIdType.MESH,
        )

    for hop in (2, 1, 3):
        col = (x + hop) % NX
        rows = pick(col)
        pick_out[hop - 1, 0] = rows[0]
        pick_out[hop - 1, 1] = rows[1]
        pick_copy(hop, col).start()
    rows = pick(x)
    pick_in[0, 0] = rows[0]
    pick_in[0, 1] = rows[1]
    for hop in range(1, NX):
        pick_copy(hop, (x + hop) % NX).wait_recv()
    for which, start in enumerate((here_a, here_b)):
        owner_x, _, _ = bank_row(start)
        row = pick_in[(x + NX - owner_x) % NX, which]
        for j in range(KVH):
            for part in range(2):
                kv_buf[j, part, pl.ds(KEYS + which * PREFIX, PREFIX), :] = row[
                    part, :, j * HD : (j + 1) * HD
                ]

    short_ones = jnp.ones((2 * PREFIX, HD), jnp.bfloat16)
    out_copies = []
    for j in range(KVH):
        keys = kv_buf[j, 0, pl.ds(KEYS, 2 * PREFIX), :]
        values = jnp.concatenate([kv_buf[j, 1, pl.ds(KEYS, 2 * PREFIX), :], short_ones], axis=1)
        for g in range(GROUPS):
            query = q_buf[:, pl.ds((j * GROUPS + g) * HD, HD)]
            scores = lax.dot_general(
                query, keys, (((1,), (1,)), ((), ())), preferred_element_type=jnp.float32
            )
            scores = scores + pbias_buf[...]
            old_top = max_buf[j, g]
            top = jnp.maximum(old_top, jnp.max(scores, axis=1, keepdims=True))
            shrink = jnp.exp2((old_top - top) * EXP_SCALE)
            weights = jnp.exp2((scores - top[:, : 2 * PREFIX]) * EXP_SCALE).astype(jnp.bfloat16)
            fresh = jnp.dot(weights, values, preferred_element_type=jnp.float32)
            mixed = acc_buf[j, g, :, pl.ds(0, HD)] * shrink + fresh[:, :HD]
            total = acc_buf[j, g, :, pl.ds(HD, HD)] * shrink + fresh[:, HD:]
            out_buf[:, pl.ds((j * GROUPS + g) * HD, HD)] = (mixed / total).astype(jnp.bfloat16)
        span = pl.ds(j * GROUPS * HD, GROUPS * HD)
        copy = pltpu.make_async_copy(out_buf.at[:, span], out_hbm.at[0, :, span], out_sem.at[j])
        copy.start()
        out_copies.append(copy)

    for j in range(KVH):

        def sent(number, j=j):
            kv_copy(j, number, 0, sibling, 1).wait_send()

        @pl.when(x < NX - 1)
        def _():
            sent(0)

        sent(1)

        @pl.when(x > 0)
        def _():
            sent(2)

        @pl.when(x == 3)
        def _():
            sent(3)

        @pl.when((row_parity == 0) & ((x == 1) | (x == 2)))
        def _():
            sent(3)
            sent(4)

        @pl.when((row_parity == 1) & (x == 0))
        def _():
            sent(2)

        @pl.when((x == 3) & (next_parity == 1))
        def _():
            sent(4)

        @pl.when((row_parity == 1) & (x == 3))
        def _():
            sent(5)

        @pl.when((x == 0) & (prev_parity == 1))
        def _():
            sent(3)

    for step in range(4):
        down_copy(step).wait_send()
        sib_copy(step, y, core).wait_send()
    for step in range(3):
        up_copy(step).wait_send()
        sib_copy(4 + step, y, core).wait_send()
    for hop in range(1, NX):
        pick_copy(hop, x).wait_send()
    for copy in out_copies:
        copy.wait()


def on_device(queries, keyvals, seg_len, seg_task, task_slot, prefix_bank):
    anywhere = pl.BlockSpec(memory_space=pl.ANY)
    bf16 = jnp.bfloat16
    return pl.pallas_call(
        kernel,
        out_shape=jax.ShapeDtypeStruct((1, T, H * HD), bf16),
        in_specs=[
            anywhere,
            anywhere,
            anywhere,
            anywhere,
            pl.BlockSpec(memory_space=pltpu.SMEM),
            anywhere,
        ],
        out_specs=anywhere,
        scratch_shapes=[
            pltpu.VMEM((T, H * HD), bf16),
            pltpu.VMEM((KVH, 2, SLOTS, HD), bf16),
            pltpu.VMEM((KVH, 2, T, HD), bf16),
            pltpu.VMEM((NY, 2, ROWS6, PREFIX, KVH * HD), bf16),
            pltpu.VMEM((NX - 1, 2, 2, PREFIX, KVH * HD), bf16),
            pltpu.VMEM((NX, 2, 2, PREFIX, KVH * HD), bf16),
            pltpu.VMEM((KVH, GROUPS, T, 2 * HD), jnp.float32),
            pltpu.VMEM((KVH, GROUPS, T, HD), jnp.float32),
            pltpu.VMEM((T, KEYS), jnp.float32),
            pltpu.VMEM((T, 2 * PREFIX), jnp.float32),
            pltpu.VMEM((T, H * HD), bf16),
            pltpu.VMEM((1, SEGS), jnp.int32),
            pltpu.VMEM((1, SEGS), jnp.int32),
            pltpu.SemaphoreType.DMA((8,)),
            pltpu.SemaphoreType.DMA((KVH,)),
            pltpu.SemaphoreType.DMA((6, KVH)),
            pltpu.SemaphoreType.DMA((4, KVH)),
            pltpu.SemaphoreType.DMA((7,)),
            pltpu.SemaphoreType.DMA((7,)),
            pltpu.SemaphoreType.DMA((7,)),
            pltpu.SemaphoreType.DMA((7,)),
            pltpu.SemaphoreType.DMA((NX - 1,)),
            pltpu.SemaphoreType.DMA((NX - 1,)),
        ],
        compiler_params=pltpu.CompilerParams(
            collective_id=0, has_side_effects=True, vmem_limit_bytes=48 << 20
        ),
    )(queries, keyvals, seg_len, seg_task, task_slot, prefix_bank)


def solution(mesh):
    in_specs = (
        P(None, ("ctx", "grp"), None),
        P(None, None, ("ctx", "grp"), None),
        P(),
        P(),
        P(),
        P(None, "grp", None, None),
    )
    out_specs = P(None, ("ctx", "grp"), None)
    return jax.shard_map(
        on_device, mesh=mesh, in_specs=in_specs, out_specs=out_specs, check_vma=False
    )
```

```python
import math

import jax
import jax.numpy as jnp
from jax import lax
from jax.experimental import pallas as pl
from jax.experimental.pallas import tpu as pltpu
from jax.sharding import PartitionSpec as P

H = 32
KVH = 4
HD = 128
GROUPS = H // KVH
T = 128
PREFIX = 16
SEGS = 512
ROWS6 = 6
HALF = ROWS6 // 2
NX = 4
NY = 8
KEYS = 4 * T
SLOTS = KEYS + 2 * PREFIX
EXP_SCALE = math.log2(math.e) / math.sqrt(HD)
NEG = -1e30
BIG = 1 << 30


def scan_lanes(row):
    lane = lax.broadcasted_iota(jnp.int32, row.shape, 1)
    step = 1
    while step < row.shape[1]:
        row = row + jnp.where(lane >= step, pltpu.roll(row, step, 1), 0)
        step *= 2
    return row


def kernel(
    q_hbm,
    kv_hbm,
    len_hbm,
    task_hbm,
    slot_smem,
    bank_hbm,
    out_hbm,
    q_buf,
    kv_buf,
    pass_buf,
    col_bank,
    pick_out,
    pick_in,
    acc_buf,
    max_buf,
    bias_buf,
    late_bias_buf,
    out_buf,
    len_buf,
    task_buf,
    local_sem,
    out_sem,
    kv_send,
    kv_recv,
    ring_send,
    ring_recv,
    sib_send,
    sib_recv,
    pick_send,
    pick_recv,
    ready_sem,
):
    ctx = lax.axis_index("ctx")
    grp = lax.axis_index("grp")
    n_ctx = lax.axis_size("ctx")
    core = ctx % 2
    x = grp % NX
    y = grp // NX
    shard = ctx * (NX * NY) + grp

    zero = shard == 0
    live = shard != 0
    twin = (ctx == 1) & (grp == 0)
    late = (ctx == 0) & (y == 0)
    mate = late & (x > 0)
    last = (ctx == n_ctx - 1) & (y == NY - 1)

    next_ctx = jnp.where(y == NY - 1, (ctx + 1) % n_ctx, ctx)
    prev_ctx = jnp.where(y == 0, (ctx + n_ctx - 1) % n_ctx, ctx)
    odd_row = core == 1
    odd_next = next_ctx % 2 == 1
    odd_prev = prev_ctx % 2 == 1
    up = (y + 1) % NY
    down = (y + NY - 1) % NY

    def in_row(col):
        return {"ctx": ctx, "grp": y * NX + col}

    def in_next(col):
        return {"ctx": next_ctx, "grp": up * NX + col}

    def in_prev(col):
        return {"ctx": prev_ctx, "grp": down * NX + col}

    def ring_node(half, row):
        skip = (ctx < 2) & (x == 0) & (row == 0)
        return {"ctx": jnp.where(skip, 1, ctx - core + half), "grp": row * NX + x}

    sibling = {"ctx": ctx + 1 - 2 * core, "grp": grp}
    first_device = {"ctx": 0, "grp": 0}
    twin_device = {"ctx": 1, "grp": 0}

    barrier = pltpu.get_barrier_semaphore()

    def greet(device):
        pl.semaphore_signal(barrier, inc=1, device_id=device, device_id_type=pl.DeviceIdType.MESH)

    row_wise = live & (x > 0) & ((y == 0) | (y == NY - 1))
    corner_down = live & (x == 0)
    corner_up = (x == NX - 1) & ~last

    @pl.when(live)
    def _():
        for hop in range(1, NX):
            col = (x + hop) % NX

            @pl.when(~(late & (col == 0)))
            def _():
                greet(in_row(col))

        greet(ring_node(core, up))
        greet(ring_node(core, down))

        @pl.when(~twin)
        def _():
            greet(sibling)

        @pl.when(mate)
        def _():
            greet(twin_device)
            greet(first_device)

        @pl.when(twin)
        def _():
            greet(ring_node(0, up))
            greet(ring_node(0, down))
            greet(first_device)
            for col in range(1, NX):
                greet({"ctx": 0, "grp": col})

        @pl.when(row_wise & (y == NY - 1))
        def _():
            greet(in_next(x))

        @pl.when(row_wise & (y == 0))
        def _():
            greet(in_prev(x))

        @pl.when(corner_down)
        def _():
            greet(in_prev(NX - 1))

        @pl.when(corner_up)
        def _():
            greet(in_next(0))

    kv_local = []
    bank_local = pltpu.make_async_copy(bank_hbm, col_bank.at[y], local_sem.at[4])
    bank_local.start()
    for j in range(KVH):
        copy = pltpu.make_async_copy(
            kv_hbm.at[:, 0, :, pl.ds(j * HD, HD)],
            kv_buf.at[j, :, pl.ds(0, T), :],
            local_sem.at[j],
        )
        copy.start()
        kv_local.append(copy)
    len_copy = pltpu.make_async_copy(len_hbm, len_buf, local_sem.at[5])
    len_copy.start()
    task_copy = pltpu.make_async_copy(task_hbm, task_buf, local_sem.at[6])
    task_copy.start()
    q_copy = pltpu.make_async_copy(q_hbm.at[0], q_buf, local_sem.at[7])
    q_copy.start()

    def one(flag):
        return jnp.where(flag, 1, 0)

    at_0, at_3 = x == 0, x == NX - 1
    not_0, not_3 = x > 0, x < NX - 1
    inner = ((x == 1) & ~late) | (x == 2)
    back_1 = at_3 & ~late
    pass_on = ~odd_row & inner | (last & (x == 2))
    detour_up = at_3 & odd_next
    relay_3 = at_3 & odd_row
    relay_1 = at_0 & odd_row
    relay_2 = ~odd_row & inner
    detour_down = at_0 & odd_prev
    relay_late = late & (x == 1)

    partners = 6 + 4 * one(twin) + one(row_wise) + one(corner_down) + one(corner_up)
    pl.semaphore_wait(barrier, jnp.where(zero, 4, partners))

    @pl.when(zero)
    def _():
        for device in ([{"ctx": 0, "grp": col} for col in range(1, NX)] + [twin_device]):
            pl.semaphore_signal(
                ready_sem, inc=1, device_id=device, device_id_type=pl.DeviceIdType.MESH
            )

    def slot_ref(j, slot):
        if slot == 4:
            return pass_buf.at[j]
        return kv_buf.at[j, :, pl.ds(slot * T, T), :]

    sends = []

    def kv_copy(j, number, source, device, target):
        return pltpu.make_async_remote_copy(
            src_ref=slot_ref(j, source),
            dst_ref=slot_ref(j, target),
            send_sem=kv_send.at[number, j],
            recv_sem=kv_recv.at[target - 1, j],
            device_id=device,
            device_id_type=pl.DeviceIdType.MESH,
        )

    def send_kv(flag, j, number, source, device, target):
        @pl.when(flag)
        def _():
            kv_copy(j, number, source, device, target).start()

        sends.append((flag, j, number))

    def wait_kv(flag, j, slot):
        @pl.when(flag)
        def _():
            kv_copy(j, 0, slot, sibling, slot).wait_recv()

    def ring_copy(half, number, part, owner, device):
        piece = col_bank.at[owner, part, pl.ds(HALF * half, HALF)]
        return pltpu.make_async_remote_copy(
            src_ref=piece,
            dst_ref=piece,
            send_sem=ring_send.at[half, number, part],
            recv_sem=ring_recv.at[half, number, part],
            device_id=device,
            device_id_type=pl.DeviceIdType.MESH,
        )

    def sib_copy(number, part, owner, half):
        piece = col_bank.at[owner, part, pl.ds(HALF * half, HALF)]
        return pltpu.make_async_remote_copy(
            src_ref=piece,
            dst_ref=piece,
            send_sem=sib_send.at[number, part],
            recv_sem=sib_recv.at[number, part],
            device_id=sibling,
            device_id_type=pl.DeviceIdType.MESH,
        )

    def down_copy(half, step, part):
        return ring_copy(half, step, part, (y + step) % NY, ring_node(half, down))

    def up_copy(half, step, part):
        return ring_copy(half, 4 + step, part, (y + NY - step) % NY, ring_node(half, up))

    bank_local.wait()

    @pl.when(live)
    def _():
        for part in range(2):
            down_copy(core, 0, part).start()
            up_copy(core, 0, part).start()

    @pl.when(twin)
    def _():
        for part in range(2):
            down_copy(0, 0, part).start()
            up_copy(0, 0, part).start()

    for j in range(KVH):
        kv_local[j].wait()
        send_kv(not_3, j, 0, 0, in_row((x + 1) % NX), 1)
        send_kv(not_0, j, 1, 0, in_next(x), 4)
        send_kv(at_0, j, 1, 0, in_row(NX - 1), 3)

    len_copy.wait()
    task_copy.wait()
    lengths = len_buf[...]
    starts = scan_lanes(lengths) - lengths
    tasks = task_buf[...]

    def segments(first):
        start_a = jnp.max(jnp.where(starts <= first, starts, 0))
        start_b = jnp.min(jnp.where(starts > first, starts, BIG))
        return start_a, start_b

    def bank_row(start):
        task = jnp.sum(jnp.where(starts == start, tasks, 0))
        row = slot_smem[task]
        owner = (row * 10923) >> 16
        return owner % NX, owner // NX, row - ROWS6 * owner

    slot_a = jnp.where(late & (x == 1), 2, 1)
    slot_b = jnp.where(late & (x == 3), 2, 3)
    slot_late = jnp.where(late & (x == 1), 1, jnp.where(late & (x == 3), 3, 2))

    here_a, here_b = segments(shard * T)
    rel_a = here_a - shard * T
    rel_b = here_b - shard * T

    query_at = lax.broadcasted_iota(jnp.int32, (T, T), 0)
    column = lax.broadcasted_iota(jnp.int32, (T, T), 1)
    earliest = jnp.where(query_at < rel_b, rel_a, rel_b)

    def block_bias(slot):
        key_at = column - slot * T
        return jnp.where((key_at >= earliest) & (key_at <= query_at), 0.0, NEG)

    bias_buf[:, pl.ds(0, T)] = block_bias(0)
    bias_buf[:, pl.ds(T, T)] = block_bias(slot_a)
    bias_buf[:, pl.ds(2 * T, T)] = block_bias(slot_b)
    late_bias_buf[:, pl.ds(0, T)] = block_bias(slot_late)
    query_at = lax.broadcasted_iota(jnp.int32, (T, 2 * PREFIX), 0)
    column_p = lax.broadcasted_iota(jnp.int32, (T, 2 * PREFIX), 1)
    late_bias_buf[:, pl.ds(T, 2 * PREFIX)] = jnp.where(
        (query_at < rel_b) == (column_p < PREFIX), 0.0, NEG
    )

    def wanted(first):
        return [bank_row(start) for start in segments(first)]

    row_wants = [wanted((shard - x + (x + hop) % NX) * T) for hop in range(NX)]

    q_copy.wait()

    def row_keys(j, blocks):
        keys = jnp.concatenate(
            [kv_buf[j, 0, pl.ds(pl.multiple_of(s * T, T), T), :] for s in blocks], axis=0
        )
        values = jnp.concatenate(
            [kv_buf[j, 1, pl.ds(pl.multiple_of(s * T, T), T), :] for s in blocks], axis=0
        )
        count = len(blocks) * T
        values = jnp.concatenate([values, jnp.ones((count, HD), jnp.bfloat16)], axis=1)
        for g in range(GROUPS):
            query = q_buf[:, pl.ds(pl.multiple_of((j * GROUPS + g) * HD, HD), HD)]
            scores = lax.dot_general(
                query, keys, (((1,), (1,)), ((), ())), preferred_element_type=jnp.float32
            )
            scores = scores + bias_buf[:, pl.ds(0, count)]
            top = jnp.max(scores, axis=1, keepdims=True)
            weights = jnp.exp2((scores - top) * EXP_SCALE).astype(jnp.bfloat16)
            acc_buf[j, g] = jnp.dot(weights, values, preferred_element_type=jnp.float32)
            max_buf[j, g] = jnp.broadcast_to(top, (T, HD))

    def first_level(j):
        wait_kv(x > 0, j, 4)
        send_kv(inner, j, 2, 4, in_row((x + 3) % NX), 3)
        send_kv(at_3, j, 2, 4, in_row(2), 3)
        send_kv(back_1, j, 3, 4, in_row(0), 1)
        wait_kv((x > 1) | ((x == 1) & ~late), j, 1)
        send_kv(pass_on, j, 3, 1, in_row((x + 1) % NX), 2)
        send_kv(detour_up, j, 4, 1, in_next(0), 2)
        wait_kv((x == 3) & ~late, j, 3)
        send_kv(relay_3, j, 5, 3, in_row(2), 2)

    def second_level(j):
        wait_kv(x == 0, j, 1)
        send_kv(relay_1, j, 2, 1, in_row(1), 2)
        wait_kv(x < 3, j, 3)
        send_kv(relay_2, j, 4, 3, in_row((x + 3) % NX), 2)
        send_kv(detour_down, j, 3, 3, in_prev(NX - 1), 2)
        wait_kv(late & (x != 2), j, 2)
        row_keys(j, (0, slot_a, slot_b))

    def ring_step(half, step, share):
        for part in range(2):
            ring_copy(half, step, part, (y + 1 + step) % NY, sibling).wait_recv()
            if step < 3:
                down_copy(half, step + 1, part).start()
            if share is not None:

                @pl.when(share)
                def _():
                    sib_copy(step, part, (y + 1 + step) % NY, half).start()

            if step < 3:
                owner = (y + NY - 1 - step) % NY
                ring_copy(half, 4 + step, part, owner, sibling).wait_recv()
                if step < 2:
                    up_copy(half, step + 1, part).start()
                if share is not None:

                    @pl.when(share)
                    def _():
                        sib_copy(4 + step, part, owner, half).start()

    def both_rings(step):
        ring_step(core, step, ~twin)

        @pl.when(twin)
        def _():
            ring_step(0, step, None)

    ring_owners = [(step, (y + 1 + step) % NY) for step in range(4)]
    ring_owners += [(4 + step, (y + NY - 1 - step) % NY) for step in range(3)]

    def pick_copy(number, slot, device):
        return pltpu.make_async_remote_copy(
            src_ref=pick_out.at[number],
            dst_ref=pick_in.at[slot],
            send_sem=pick_send.at[number],
            recv_sem=pick_recv.at[slot],
            device_id=device,
            device_id_type=pl.DeviceIdType.MESH,
        )

    def pick(ref, place, wants):
        for which in range(2):
            _, owner_y, row = wants[which]
            ref[place, which] = col_bank[owner_y, :, row]

    @pl.when(live)
    def _():
        both_rings(0)
        first_level(0)
        first_level(1)
        both_rings(1)
        first_level(2)
        second_level(0)
        first_level(3)
        both_rings(2)
        second_level(1)
        second_level(2)
        both_rings(3)
        second_level(3)

        @pl.when(~twin)
        def _():
            for number, owner in ring_owners:
                for part in range(2):
                    sib_copy(number, part, owner, 1 - core).wait_recv()

        for hop in (2, 1, 3):
            col = (x + hop) % NX

            @pl.when(~(late & (col == 0)))
            def _():
                pick(pick_out, hop - 1, row_wants[hop])
                pick_copy(hop - 1, hop, in_row(col)).start()

        pick(pick_in, 0, row_wants[0])

        @pl.when(twin)
        def _():
            for col in range(NX):
                pick(pick_out, NX - 1 + col, wanted(col * T))
            for col in range(1, NX):
                pick_copy(NX - 1 + col, col, {"ctx": 0, "grp": col}).start()
            pl.semaphore_wait(ready_sem, 1)
            pick_copy(NX - 1, 0, first_device).start()

        @pl.when(mate)
        def _():
            pl.semaphore_wait(ready_sem, 1)
            for hop in range(1, NX):

                @pl.when((x + hop) % NX == 0)
                def _():
                    pick(pick_out, hop - 1, row_wants[hop])
                    pick_copy(hop - 1, hop, first_device).start()

    @pl.when(zero)
    def _():
        for j in range(KVH):
            kv_buf[j, :, pl.ds(2 * T, T), :] = jnp.zeros((2, T, HD), jnp.bfloat16)
            row_keys(j, (0,))
        pick_copy(0, 0, twin_device).wait_recv()

    for hop in range(1, NX):
        pick_copy(0, hop, sibling).wait_recv()
    for which in range(2):
        owner_x, _, _ = row_wants[0][which]
        row = pick_in[(x + NX - owner_x) % NX, which]
        for j in range(KVH):
            for part in range(2):
                kv_buf[j, part, pl.ds(KEYS + which * PREFIX, PREFIX), :] = row[
                    part, :, j * HD : (j + 1) * HD
                ]

    out_copies = []
    for j in range(KVH):

        @pl.when(live)
        def _():
            pltpu.make_async_remote_copy(
                src_ref=kv_buf.at[j, :, pl.ds(0, T), :],
                dst_ref=kv_buf.at[j, :, pl.ds(slot_late * T, T), :],
                send_sem=kv_send.at[0, j],
                recv_sem=kv_recv.at[slot_late - 1, j],
                device_id=sibling,
                device_id_type=pl.DeviceIdType.MESH,
            ).wait_recv()

        send_kv(relay_late, j, 3, 1, in_row(2), 2)
        due = pl.ds(pl.multiple_of(slot_late * T, T), T)
        prefix = pl.ds(KEYS, 2 * PREFIX)
        keys = jnp.concatenate([kv_buf[j, 0, due, :], kv_buf[j, 0, prefix, :]], axis=0)
        values = jnp.concatenate([kv_buf[j, 1, due, :], kv_buf[j, 1, prefix, :]], axis=0)
        values = jnp.concatenate(
            [values, jnp.ones((T + 2 * PREFIX, HD), jnp.bfloat16)], axis=1
        )
        for g in range(GROUPS):
            query = q_buf[:, pl.ds((j * GROUPS + g) * HD, HD)]
            scores = lax.dot_general(
                query, keys, (((1,), (1,)), ((), ())), preferred_element_type=jnp.float32
            )
            scores = scores + late_bias_buf[...]
            old_top = max_buf[j, g]
            top = jnp.maximum(old_top, jnp.max(scores, axis=1, keepdims=True))
            shrink = jnp.exp2((old_top - top) * EXP_SCALE)
            tops = jnp.concatenate([top, top[:, : 2 * PREFIX]], axis=1)
            weights = jnp.exp2((scores - tops) * EXP_SCALE).astype(jnp.bfloat16)
            fresh = jnp.dot(weights, values, preferred_element_type=jnp.float32)
            mixed = acc_buf[j, g, :, pl.ds(0, HD)] * shrink + fresh[:, :HD]
            total = acc_buf[j, g, :, pl.ds(HD, HD)] * shrink + fresh[:, HD:]
            out_buf[:, pl.ds((j * GROUPS + g) * HD, HD)] = (mixed / total).astype(jnp.bfloat16)
        span = pl.ds(j * GROUPS * HD, GROUPS * HD)
        copy = pltpu.make_async_copy(out_buf.at[:, span], out_hbm.at[0, :, span], out_sem.at[j])
        copy.start()
        out_copies.append(copy)

    for flag, j, number in sends:
        own = number < 2
        keep = flag if own else flag & live

        @pl.when(keep)
        def _():
            kv_copy(j, number, 0, sibling, 1).wait_send()

    @pl.when(live)
    def _():
        for part in range(2):
            for step in range(4):
                down_copy(core, step, part).wait_send()
            for step in range(3):
                up_copy(core, step, part).wait_send()
        for hop in range(1, NX):
            pick_copy(hop - 1, hop, sibling).wait_send()

        @pl.when(~twin)
        def _():
            for number, owner in ring_owners:
                for part in range(2):
                    sib_copy(number, part, owner, core).wait_send()

        @pl.when(twin)
        def _():
            for part in range(2):
                for step in range(4):
                    down_copy(0, step, part).wait_send()
                for step in range(3):
                    up_copy(0, step, part).wait_send()
            for col in range(NX):
                pick_copy(NX - 1 + col, col, first_device).wait_send()

    for copy in out_copies:
        copy.wait()


def on_device(queries, keyvals, seg_len, seg_task, task_slot, prefix_bank):
    anywhere = pl.BlockSpec(memory_space=pl.ANY)
    bf16 = jnp.bfloat16
    return pl.pallas_call(
        kernel,
        out_shape=jax.ShapeDtypeStruct((1, T, H * HD), bf16),
        in_specs=[
            anywhere,
            anywhere,
            anywhere,
            anywhere,
            pl.BlockSpec(memory_space=pltpu.SMEM),
            anywhere,
        ],
        out_specs=anywhere,
        scratch_shapes=[
            pltpu.VMEM((T, H * HD), bf16),
            pltpu.VMEM((KVH, 2, SLOTS, HD), bf16),
            pltpu.VMEM((KVH, 2, T, HD), bf16),
            pltpu.VMEM((NY, 2, ROWS6, PREFIX, KVH * HD), bf16),
            pltpu.VMEM((2 * NX - 1, 2, 2, PREFIX, KVH * HD), bf16),
            pltpu.VMEM((NX, 2, 2, PREFIX, KVH * HD), bf16),
            pltpu.VMEM((KVH, GROUPS, T, 2 * HD), jnp.float32),
            pltpu.VMEM((KVH, GROUPS, T, HD), jnp.float32),
            pltpu.VMEM((T, KEYS - T), jnp.float32),
            pltpu.VMEM((T, T + 2 * PREFIX), jnp.float32),
            pltpu.VMEM((T, H * HD), bf16),
            pltpu.VMEM((1, SEGS), jnp.int32),
            pltpu.VMEM((1, SEGS), jnp.int32),
            pltpu.SemaphoreType.DMA((8,)),
            pltpu.SemaphoreType.DMA((KVH,)),
            pltpu.SemaphoreType.DMA((6, KVH)),
            pltpu.SemaphoreType.DMA((4, KVH)),
            pltpu.SemaphoreType.DMA((2, 7, 2)),
            pltpu.SemaphoreType.DMA((2, 7, 2)),
            pltpu.SemaphoreType.DMA((7, 2)),
            pltpu.SemaphoreType.DMA((7, 2)),
            pltpu.SemaphoreType.DMA((2 * NX - 1,)),
            pltpu.SemaphoreType.DMA((NX,)),
            pltpu.SemaphoreType.REGULAR,
        ],
        compiler_params=pltpu.CompilerParams(
            collective_id=0, has_side_effects=True, vmem_limit_bytes=67043328
        ),
    )(queries, keyvals, seg_len, seg_task, task_slot, prefix_bank)


def solution(mesh):
    in_specs = (
        P(None, ("ctx", "grp"), None),
        P(None, None, ("ctx", "grp"), None),
        P(),
        P(),
        P(),
        P(None, "grp", None, None),
    )
    out_specs = P(None, ("ctx", "grp"), None)
    return jax.shard_map(
        on_device, mesh=mesh, in_specs=in_specs, out_specs=out_specs, check_vma=False
    )
```

```python
import math

import jax
import jax.numpy as jnp
from jax import lax
from jax.experimental import pallas as pl
from jax.experimental.pallas import tpu as pltpu
from jax.sharding import PartitionSpec as P

H = 32
KVH = 4
HD = 128
GROUPS = H // KVH
T = 128
PREFIX = 16
SEGS = 512
ROWS6 = 6
HALF = ROWS6 // 2
NX = 4
NY = 8
KEYS = 4 * T
SLOTS = KEYS + 2 * PREFIX
EXP_SCALE = math.log2(math.e) / math.sqrt(HD)
NEG = -1e30
BIG = 1 << 30


def scan_lanes(row):
    lane = lax.broadcasted_iota(jnp.int32, row.shape, 1)
    step = 1
    while step < row.shape[1]:
        row = row + jnp.where(lane >= step, pltpu.roll(row, step, 1), 0)
        step *= 2
    return row


def kernel(
    q_hbm,
    kv_hbm,
    len_hbm,
    task_hbm,
    slot_smem,
    bank_hbm,
    out_hbm,
    q_buf,
    kv_buf,
    pass_buf,
    col_bank,
    pick_out,
    pick_in,
    acc_buf,
    max_buf,
    bias_buf,
    late_bias_buf,
    out_buf,
    len_buf,
    task_buf,
    local_sem,
    out_sem,
    kv_send,
    kv_recv,
    ring_send,
    ring_recv,
    sib_send,
    sib_recv,
    pick_send,
    pick_recv,
    ready_sem,
):
    ctx = lax.axis_index("ctx")
    grp = lax.axis_index("grp")
    n_ctx = lax.axis_size("ctx")
    core = ctx % 2
    x = grp % NX
    y = grp // NX
    shard = ctx * (NX * NY) + grp

    zero = shard == 0
    live = shard != 0
    twin = (ctx == 1) & (grp == 0)
    late = (ctx == 0) & (y == 0)
    mate = late & (x > 0)
    last = (ctx == n_ctx - 1) & (y == NY - 1)

    next_ctx = jnp.where(y == NY - 1, (ctx + 1) % n_ctx, ctx)
    prev_ctx = jnp.where(y == 0, (ctx + n_ctx - 1) % n_ctx, ctx)
    odd_row = core == 1
    odd_next = next_ctx % 2 == 1
    odd_prev = prev_ctx % 2 == 1
    up = (y + 1) % NY
    down = (y + NY - 1) % NY

    def in_row(col):
        return {"ctx": ctx, "grp": y * NX + col}

    def in_next(col):
        return {"ctx": next_ctx, "grp": up * NX + col}

    def in_prev(col):
        return {"ctx": prev_ctx, "grp": down * NX + col}

    def ring_node(half, row):
        skip = (ctx < 2) & (x == 0) & (row == 0)
        return {"ctx": jnp.where(skip, 1, ctx - core + half), "grp": row * NX + x}

    sibling = {"ctx": ctx + 1 - 2 * core, "grp": grp}
    first_device = {"ctx": 0, "grp": 0}
    twin_device = {"ctx": 1, "grp": 0}

    barrier = pltpu.get_barrier_semaphore()

    def greet(device):
        pl.semaphore_signal(barrier, inc=1, device_id=device, device_id_type=pl.DeviceIdType.MESH)

    wrap_up = (x > 0) & (y == NY - 1) & ~last
    wrap_down = (x > 0) & (y == 0) & ~late
    corner_down = live & (x == 0)
    corner_up = (x == NX - 1) & ~last

    @pl.when(live)
    def _():
        for hop in range(1, NX):
            col = (x + hop) % NX

            @pl.when(~(late & (col == 0)))
            def _():
                greet(in_row(col))

        greet(ring_node(core, up))
        greet(ring_node(core, down))

        @pl.when(~twin)
        def _():
            greet(sibling)

        @pl.when(mate)
        def _():
            greet(twin_device)
            greet(first_device)

        @pl.when(twin)
        def _():
            greet(ring_node(0, up))
            greet(ring_node(0, down))
            greet(first_device)
            for col in range(1, NX):
                greet({"ctx": 0, "grp": col})

        @pl.when(wrap_up)
        def _():
            greet(in_next(x))

        @pl.when(wrap_down)
        def _():
            greet(in_prev(x))

        @pl.when(corner_down)
        def _():
            greet(in_prev(NX - 1))

        @pl.when(corner_up)
        def _():
            greet(in_next(0))

    kv_local = []
    bank_local = pltpu.make_async_copy(bank_hbm, col_bank.at[y], local_sem.at[4])
    bank_local.start()
    for j in range(KVH):
        copy = pltpu.make_async_copy(
            kv_hbm.at[:, 0, :, pl.ds(j * HD, HD)],
            kv_buf.at[j, :, pl.ds(0, T), :],
            local_sem.at[j],
        )
        copy.start()
        kv_local.append(copy)
    len_copy = pltpu.make_async_copy(len_hbm, len_buf, local_sem.at[5])
    len_copy.start()
    task_copy = pltpu.make_async_copy(task_hbm, task_buf, local_sem.at[6])
    task_copy.start()
    q_copy = pltpu.make_async_copy(q_hbm.at[0], q_buf, local_sem.at[7])
    q_copy.start()

    def one(flag):
        return jnp.where(flag, 1, 0)

    at_0, at_3 = x == 0, x == NX - 1
    not_3 = x < NX - 1
    give_up = (x > 0) & ~last
    take_up = (x > 0) & ~late
    inner = ((x == 1) | (x == 2)) & ~late
    back = at_3 & ~late
    pass_on = ~odd_row & (((x == 1) & ~late) | (x == 2)) | (last & (x == 2))
    detour_up = at_3 & odd_next
    relay_3 = at_3 & odd_row
    relay_1 = at_0 & odd_row
    relay_2 = ~odd_row & inner
    detour_down = at_0 & odd_prev
    relay_late = late & (x == 1)

    partners = 6 + 4 * one(twin) + one(wrap_up | wrap_down) + one(corner_down) + one(corner_up)
    pl.semaphore_wait(barrier, jnp.where(zero, 4, partners))

    @pl.when(zero)
    def _():
        for device in ([{"ctx": 0, "grp": col} for col in range(1, NX)] + [twin_device]):
            pl.semaphore_signal(
                ready_sem, inc=1, device_id=device, device_id_type=pl.DeviceIdType.MESH
            )

    def slot_ref(j, slot):
        if slot == 4:
            return pass_buf.at[j]
        return kv_buf.at[j, :, pl.ds(slot * T, T), :]

    sends = []

    def kv_copy(j, number, source, device, target):
        return pltpu.make_async_remote_copy(
            src_ref=slot_ref(j, source),
            dst_ref=slot_ref(j, target),
            send_sem=kv_send.at[number, j],
            recv_sem=kv_recv.at[target - 1, j],
            device_id=device,
            device_id_type=pl.DeviceIdType.MESH,
        )

    def send_kv(flag, j, number, source, device, target):
        @pl.when(flag)
        def _():
            kv_copy(j, number, source, device, target).start()

        sends.append((flag, j, number))

    def wait_kv(flag, j, slot):
        @pl.when(flag)
        def _():
            kv_copy(j, 0, slot, sibling, slot).wait_recv()

    def ring_copy(half, number, part, owner, device):
        piece = col_bank.at[owner, :, HALF * half + part]
        return pltpu.make_async_remote_copy(
            src_ref=piece,
            dst_ref=piece,
            send_sem=ring_send.at[half, number, part],
            recv_sem=ring_recv.at[half, number, part],
            device_id=device,
            device_id_type=pl.DeviceIdType.MESH,
        )

    def sib_copy(number, part, owner, half):
        piece = col_bank.at[owner, :, HALF * half + part]
        return pltpu.make_async_remote_copy(
            src_ref=piece,
            dst_ref=piece,
            send_sem=sib_send.at[number, part],
            recv_sem=sib_recv.at[number, part],
            device_id=sibling,
            device_id_type=pl.DeviceIdType.MESH,
        )

    def down_copy(half, step, part):
        return ring_copy(half, step, part, (y + step) % NY, ring_node(half, down))

    def up_copy(half, step, part):
        return ring_copy(half, 4 + step, part, (y + NY - step) % NY, ring_node(half, up))

    bank_local.wait()

    @pl.when(live)
    def _():
        for part in range(HALF):
            down_copy(core, 0, part).start()

    @pl.when(twin)
    def _():
        for part in range(HALF):
            down_copy(0, 0, part).start()

    def give(j):
        send_kv(give_up, j, 1, 0, in_next(x), 4)

    kv_local[0].wait()
    give(0)

    @pl.when(live)
    def _():
        for part in range(HALF):
            up_copy(core, 0, part).start()

    @pl.when(twin)
    def _():
        for part in range(HALF):
            up_copy(0, 0, part).start()

    for j in range(KVH):
        if j > 0:
            kv_local[j].wait()
        send_kv(not_3, j, 0, 0, in_row((x + 1) % NX), 1)
        send_kv(at_0, j, 1, 0, in_row(NX - 1), 3)
    give(1)

    def first_level(j):
        wait_kv(take_up, j, 4)
        send_kv(inner, j, 2, 4, in_row((x + 3) % NX), 3)
        send_kv(back, j, 2, 4, in_row(2), 3)
        send_kv(back, j, 3, 4, in_row(0), 1)
        wait_kv((x > 1) | ((x == 1) & ~late), j, 1)
        send_kv(pass_on, j, 3, 1, in_row((x + 1) % NX), 2)
        send_kv(detour_up, j, 4, 1, in_next(0), 2)
        wait_kv((x == 3) & ~late, j, 3)
        send_kv(relay_3, j, 5, 3, in_row(2), 2)

    def second_level(j):
        wait_kv(x == 0, j, 1)
        send_kv(relay_1, j, 2, 1, in_row(1), 2)
        wait_kv((x < 3) & ~late, j, 3)
        send_kv(relay_2, j, 4, 3, in_row((x + 3) % NX), 2)
        send_kv(detour_down, j, 3, 3, in_prev(NX - 1), 2)
        wait_kv(late & at_3, j, 2)

    def ring_step(half, step, share):
        for part in range(HALF):
            ring_copy(half, step, part, (y + 1 + step) % NY, sibling).wait_recv()
            if step < 3:
                down_copy(half, step + 1, part).start()
            if share is not None:

                @pl.when(share)
                def _():
                    sib_copy(step, part, (y + 1 + step) % NY, half).start()

            if step < 3:
                owner = (y + NY - 1 - step) % NY
                ring_copy(half, 4 + step, part, owner, sibling).wait_recv()
                if step < 2:
                    up_copy(half, step + 1, part).start()
                if share is not None:

                    @pl.when(share)
                    def _():
                        sib_copy(4 + step, part, owner, half).start()

    def both_rings(step):
        ring_step(core, step, ~twin)

        @pl.when(twin)
        def _():
            ring_step(0, step, None)

    ring_owners = [(step, (y + 1 + step) % NY) for step in range(4)]
    ring_owners += [(4 + step, (y + NY - 1 - step) % NY) for step in range(3)]

    def pick_copy(number, slot, device):
        return pltpu.make_async_remote_copy(
            src_ref=pick_out.at[number],
            dst_ref=pick_in.at[slot],
            send_sem=pick_send.at[number],
            recv_sem=pick_recv.at[slot],
            device_id=device,
            device_id_type=pl.DeviceIdType.MESH,
        )

    def pick(ref, place, wants):
        for which in range(2):
            _, owner_y, row = wants[which]
            ref[place, which] = col_bank[owner_y, :, row]

    @pl.when(live)
    def _():
        both_rings(0)

    give(2)

    @pl.when(live)
    def _():
        first_level(0)
        first_level(1)

    len_copy.wait()
    task_copy.wait()
    lengths = len_buf[...]
    starts = scan_lanes(lengths) - lengths
    tasks = task_buf[...]

    def segments(first):
        start_a = jnp.max(jnp.where(starts <= first, starts, 0))
        start_b = jnp.min(jnp.where(starts > first, starts, BIG))
        return start_a, start_b

    def bank_row(start):
        task = jnp.sum(jnp.where(starts == start, tasks, 0))
        row = slot_smem[task]
        owner = (row * 10923) >> 16
        return owner % NX, owner // NX, row - ROWS6 * owner

    slot_a = jnp.where(late & (x == 1), 2, 1)
    slot_b = jnp.where(late & (x == 3), 2, 3)
    slot_late = jnp.where(late & (x == 1), 1, jnp.where(late & (x == 3), 3, 2))

    here_a, here_b = segments(shard * T)
    rel_a = here_a - shard * T
    rel_b = here_b - shard * T

    query_at = lax.broadcasted_iota(jnp.int32, (T, T), 0)
    column = lax.broadcasted_iota(jnp.int32, (T, T), 1)
    earliest = jnp.where(query_at < rel_b, rel_a, rel_b)

    def block_bias(slot):
        key_at = column - slot * T
        return jnp.where((key_at >= earliest) & (key_at <= query_at), 0.0, NEG)

    bias_buf[:, pl.ds(0, T)] = block_bias(0)
    bias_buf[:, pl.ds(T, T)] = block_bias(slot_a)
    bias_buf[:, pl.ds(2 * T, T)] = block_bias(slot_b)
    bias_buf[:, pl.ds(3 * T, T)] = block_bias(slot_late)
    late_bias_buf[:, pl.ds(0, T)] = block_bias(slot_late)
    query_at = lax.broadcasted_iota(jnp.int32, (T, 2 * PREFIX), 0)
    column_p = lax.broadcasted_iota(jnp.int32, (T, 2 * PREFIX), 1)
    late_bias_buf[:, pl.ds(T, 2 * PREFIX)] = jnp.where(
        (query_at < rel_b) == (column_p < PREFIX), 0.0, NEG
    )

    def wanted(first):
        return [bank_row(start) for start in segments(first)]


    @pl.when(live)
    def _():
        both_rings(1)

    give(3)

    @pl.when(live)
    def _():
        second_level(0)
        first_level(2)

    row_wants = [wanted((shard - x + (x + hop) % NX) * T) for hop in range(NX)]

    for slot in (2, 3):

        @pl.when(late & (x < slot))
        def _():
            for j in range(KVH):
                kv_buf[j, :, pl.ds(slot * T, T), :] = jnp.zeros((2, T, HD), jnp.bfloat16)

    @pl.when(live)
    def _():
        both_rings(2)
        second_level(1)
        first_level(3)
        second_level(2)
        both_rings(3)

        @pl.when(~twin)
        def _():
            for number, owner in ring_owners:
                for part in range(HALF):
                    sib_copy(number, part, owner, 1 - core).wait_recv()

        for hop in (2, 1, 3):
            col = (x + hop) % NX

            @pl.when(~(late & (col == 0)))
            def _():
                pick(pick_out, hop - 1, row_wants[hop])
                pick_copy(hop - 1, hop, in_row(col)).start()

        pick(pick_in, 0, row_wants[0])

        second_level(3)

        @pl.when(twin)
        def _():
            for col in range(NX):
                pick(pick_out, NX - 1 + col, wanted(col * T))
            for col in range(1, NX):
                pick_copy(NX - 1 + col, col, {"ctx": 0, "grp": col}).start()
            pl.semaphore_wait(ready_sem, 1)
            pick_copy(NX - 1, 0, first_device).start()

        @pl.when(mate)
        def _():
            pl.semaphore_wait(ready_sem, 1)
            for hop in range(1, NX):

                @pl.when((x + hop) % NX == 0)
                def _():
                    pick(pick_out, hop - 1, row_wants[hop])
                    pick_copy(hop - 1, hop, first_device).start()

    q_copy.wait()

    def row_keys(j, blocks):
        keys = jnp.concatenate(
            [kv_buf[j, 0, pl.ds(pl.multiple_of(s * T, T), T), :] for s in blocks], axis=0
        )
        values = jnp.concatenate(
            [kv_buf[j, 1, pl.ds(pl.multiple_of(s * T, T), T), :] for s in blocks], axis=0
        )
        count = len(blocks) * T
        values = jnp.concatenate([values, jnp.ones((count, HD), jnp.bfloat16)], axis=1)
        for g in range(GROUPS):
            query = q_buf[:, pl.ds(pl.multiple_of((j * GROUPS + g) * HD, HD), HD)]
            scores = lax.dot_general(
                query, keys, (((1,), (1,)), ((), ())), preferred_element_type=jnp.float32
            )
            scores = scores + bias_buf[:, pl.ds(0, count)]
            top = jnp.max(scores, axis=1, keepdims=True)
            weights = jnp.exp2((scores - top) * EXP_SCALE).astype(jnp.bfloat16)
            acc_buf[j, g] = jnp.dot(weights, values, preferred_element_type=jnp.float32)
            max_buf[j, g] = jnp.broadcast_to(top, (T, HD))

    normal = ~late

    @pl.when(normal)
    def _():
        for j in range(KVH):
            wait_kv(normal, j, 2)
            row_keys(j, (0, 1, 3, 2))

    @pl.when(mate)
    def _():
        @pl.loop(0, KVH)
        def _(j):
            row_keys(j, (0, slot_a, slot_b))

    @pl.when(zero)
    def _():
        @pl.loop(0, KVH)
        def _(j):
            row_keys(j, (0,))

        pick_copy(0, 0, twin_device).wait_recv()

    for hop in range(1, NX):
        pick_copy(0, hop, sibling).wait_recv()
    for which in range(2):
        owner_x, _, _ = row_wants[0][which]
        row = pick_in[(x + NX - owner_x) % NX, which]
        for j in range(KVH):
            for part in range(2):
                kv_buf[j, part, pl.ds(KEYS + which * PREFIX, PREFIX), :] = row[
                    part, :, j * HD : (j + 1) * HD
                ]

    def finish(j, due):
        prefix = pl.ds(KEYS, 2 * PREFIX)
        keys = kv_buf[j, 0, prefix, :]
        values = kv_buf[j, 1, prefix, :]
        bias = late_bias_buf[:, pl.ds(T, 2 * PREFIX)]
        if due:
            block = pl.ds(pl.multiple_of(slot_late * T, T), T)
            keys = jnp.concatenate([kv_buf[j, 0, block, :], keys], axis=0)
            values = jnp.concatenate([kv_buf[j, 1, block, :], values], axis=0)
            bias = late_bias_buf[...]
        count = values.shape[0]
        values = jnp.concatenate([values, jnp.ones((count, HD), jnp.bfloat16)], axis=1)
        for g in range(GROUPS):
            head = pl.ds(pl.multiple_of((j * GROUPS + g) * HD, HD), HD)
            scores = lax.dot_general(
                q_buf[:, head], keys, (((1,), (1,)), ((), ())), preferred_element_type=jnp.float32
            )
            scores = scores + bias
            old_top = max_buf[j, g]
            top = jnp.maximum(old_top, jnp.max(scores, axis=1, keepdims=True))
            shrink = jnp.exp2((old_top - top) * EXP_SCALE)
            tops = top[:, : 2 * PREFIX]
            if due:
                tops = jnp.concatenate([top, tops], axis=1)
            weights = jnp.exp2((scores - tops) * EXP_SCALE).astype(jnp.bfloat16)
            fresh = jnp.dot(weights, values, preferred_element_type=jnp.float32)
            mixed = acc_buf[j, g, :, pl.ds(0, HD)] * shrink + fresh[:, :HD]
            total = acc_buf[j, g, :, pl.ds(HD, HD)] * shrink + fresh[:, HD:]
            out_buf[:, head] = (mixed / total).astype(jnp.bfloat16)
        span = pl.ds(pl.multiple_of(j * GROUPS * HD, GROUPS * HD), GROUPS * HD)
        pltpu.make_async_copy(out_buf.at[:, span], out_hbm.at[0, :, span], out_sem.at[j]).start()

    @pl.when(normal)
    def _():
        for j in range(KVH):
            finish(j, False)

    @pl.when(late)
    def _():
        @pl.loop(0, KVH)
        def _(j):
            @pl.when(mate)
            def _():
                pltpu.make_async_remote_copy(
                    src_ref=kv_buf.at[j, :, pl.ds(0, T), :],
                    dst_ref=kv_buf.at[j, :, pl.ds(slot_late * T, T), :],
                    send_sem=kv_send.at[0, j],
                    recv_sem=kv_recv.at[slot_late - 1, j],
                    device_id=sibling,
                    device_id_type=pl.DeviceIdType.MESH,
                ).wait_recv()

            @pl.when(relay_late)
            def _():
                kv_copy(j, 3, 1, in_row(2), 2).start()

            finish(j, True)

    sends.extend((relay_late, j, 3) for j in range(KVH))

    for flag, j, number in sends:
        own = number < 2
        keep = flag if own else flag & live

        @pl.when(keep)
        def _():
            kv_copy(j, number, 0, sibling, 1).wait_send()

    @pl.when(live)
    def _():
        for part in range(HALF):
            for step in range(4):
                down_copy(core, step, part).wait_send()
            for step in range(3):
                up_copy(core, step, part).wait_send()
        for hop in range(1, NX):
            pick_copy(hop - 1, hop, sibling).wait_send()

        @pl.when(~twin)
        def _():
            for number, owner in ring_owners:
                for part in range(HALF):
                    sib_copy(number, part, owner, core).wait_send()

        @pl.when(twin)
        def _():
            for part in range(HALF):
                for step in range(4):
                    down_copy(0, step, part).wait_send()
                for step in range(3):
                    up_copy(0, step, part).wait_send()
            for col in range(NX):
                pick_copy(NX - 1 + col, col, first_device).wait_send()

    for j in range(KVH):
        span = pl.ds(j * GROUPS * HD, GROUPS * HD)
        pltpu.make_async_copy(out_buf.at[:, span], out_hbm.at[0, :, span], out_sem.at[j]).wait()


def on_device(queries, keyvals, seg_len, seg_task, task_slot, prefix_bank):
    anywhere = pl.BlockSpec(memory_space=pl.ANY)
    bf16 = jnp.bfloat16
    return pl.pallas_call(
        kernel,
        out_shape=jax.ShapeDtypeStruct((1, T, H * HD), bf16),
        in_specs=[
            anywhere,
            anywhere,
            anywhere,
            anywhere,
            pl.BlockSpec(memory_space=pltpu.SMEM),
            anywhere,
        ],
        out_specs=anywhere,
        scratch_shapes=[
            pltpu.VMEM((T, H * HD), bf16),
            pltpu.VMEM((KVH, 2, SLOTS, HD), bf16),
            pltpu.VMEM((KVH, 2, T, HD), bf16),
            pltpu.VMEM((NY, 2, ROWS6, PREFIX, KVH * HD), bf16),
            pltpu.VMEM((2 * NX - 1, 2, 2, PREFIX, KVH * HD), bf16),
            pltpu.VMEM((NX, 2, 2, PREFIX, KVH * HD), bf16),
            pltpu.VMEM((KVH, GROUPS, T, 2 * HD), jnp.float32),
            pltpu.VMEM((KVH, GROUPS, T, HD), jnp.float32),
            pltpu.VMEM((T, KEYS), jnp.float32),
            pltpu.VMEM((T, T + 2 * PREFIX), jnp.float32),
            pltpu.VMEM((T, H * HD), bf16),
            pltpu.VMEM((1, SEGS), jnp.int32),
            pltpu.VMEM((1, SEGS), jnp.int32),
            pltpu.SemaphoreType.DMA((8,)),
            pltpu.SemaphoreType.DMA((KVH,)),
            pltpu.SemaphoreType.DMA((6, KVH)),
            pltpu.SemaphoreType.DMA((4, KVH)),
            pltpu.SemaphoreType.DMA((2, 7, HALF)),
            pltpu.SemaphoreType.DMA((2, 7, HALF)),
            pltpu.SemaphoreType.DMA((7, HALF)),
            pltpu.SemaphoreType.DMA((7, HALF)),
            pltpu.SemaphoreType.DMA((2 * NX - 1,)),
            pltpu.SemaphoreType.DMA((NX,)),
            pltpu.SemaphoreType.REGULAR,
        ],
        compiler_params=pltpu.CompilerParams(
            collective_id=0, has_side_effects=True, vmem_limit_bytes=67043328
        ),
    )(queries, keyvals, seg_len, seg_task, task_slot, prefix_bank)


def solution(mesh):
    in_specs = (
        P(None, ("ctx", "grp"), None),
        P(None, None, ("ctx", "grp"), None),
        P(),
        P(),
        P(),
        P(None, "grp", None, None),
    )
    out_specs = P(None, ("ctx", "grp"), None)
    return jax.shard_map(
        on_device, mesh=mesh, in_specs=in_specs, out_specs=out_specs, check_vma=False
    )
```

```python
import math

import jax
import jax.numpy as jnp
from jax import lax
from jax.experimental import pallas as pl
from jax.experimental.pallas import tpu as pltpu
from jax.sharding import PartitionSpec as P

H = 32
KVH = 4
HD = 128
GROUPS = H // KVH
T = 128
PREFIX = 16
SEGS = 512
ROWS6 = 6
HALF = ROWS6 // 2
NX = 4
NY = 8
KEYS = 4 * T
SLOTS = KEYS + 2 * PREFIX
EXP_SCALE = math.log2(math.e) / math.sqrt(HD)
NEG = -1e30
BIG = 1 << 30


def scan_lanes(row):
    lane = lax.broadcasted_iota(jnp.int32, row.shape, 1)
    step = 1
    while step < row.shape[1]:
        row = row + jnp.where(lane >= step, pltpu.roll(row, step, 1), 0)
        step *= 2
    return row


def kernel(
    q_hbm,
    kv_hbm,
    len_hbm,
    task_hbm,
    slot_smem,
    bank_hbm,
    out_hbm,
    q_buf,
    kv_buf,
    pass_buf,
    col_bank,
    pick_out,
    pick_in,
    acc_buf,
    max_buf,
    bias_buf,
    late_bias_buf,
    out_buf,
    len_buf,
    task_buf,
    local_sem,
    out_sem,
    kv_send,
    kv_recv,
    ring_send,
    ring_recv,
    sib_send,
    sib_recv,
    cross_send,
    cross_recv,
    pick_send,
    pick_recv,
    ready_sem,
):
    ctx = lax.axis_index("ctx")
    grp = lax.axis_index("grp")
    n_ctx = lax.axis_size("ctx")
    core = ctx % 2
    x = grp % NX
    y = grp // NX
    shard = ctx * (NX * NY) + grp

    zero = shard == 0
    live = shard != 0
    twin = (ctx == 1) & (grp == 0)
    late = (ctx == 0) & (y == 0)
    mate = late & (x > 0)
    last = (ctx == n_ctx - 1) & (y == NY - 1)

    next_ctx = jnp.where(y == NY - 1, (ctx + 1) % n_ctx, ctx)
    prev_ctx = jnp.where(y == 0, (ctx + n_ctx - 1) % n_ctx, ctx)
    pair = (ctx // 2) % 2
    up = (y + 1) % NY
    down = (y + NY - 1) % NY

    def in_row(col):
        return {"ctx": ctx, "grp": y * NX + col}

    def in_next(col):
        return {"ctx": next_ctx, "grp": up * NX + col}

    def in_prev(col):
        return {"ctx": prev_ctx, "grp": down * NX + col}

    def ring_node(half, row):
        skip = (ctx < 2) & (x == 0) & (row == 0)
        return {"ctx": jnp.where(skip, 1, ctx - core + half), "grp": row * NX + x}

    def cross_node(half):
        far = ctx - core + half + 2 - 4 * pair
        return {"ctx": jnp.where((far == 0) & (grp == 0), 1, far), "grp": grp}

    sibling = {"ctx": ctx + 1 - 2 * core, "grp": grp}
    first_device = {"ctx": 0, "grp": 0}
    twin_device = {"ctx": 1, "grp": 0}

    barrier = pltpu.get_barrier_semaphore()

    def greet(device):
        pl.semaphore_signal(barrier, inc=1, device_id=device, device_id_type=pl.DeviceIdType.MESH)

    wrap_up = (x > 0) & (y == NY - 1) & ~last
    wrap_down = (x > 0) & (y == 0) & ~late

    @pl.when(live)
    def _():
        for hop in range(1, NX):
            col = (x + hop) % NX

            @pl.when(~(late & (col == 0)))
            def _():
                greet(in_row(col))

        greet(ring_node(core, up))
        greet(ring_node(core, down))
        greet(cross_node(core))

        @pl.when(~twin)
        def _():
            greet(sibling)

        @pl.when(mate)
        def _():
            greet(twin_device)
            greet(first_device)

        @pl.when(twin)
        def _():
            greet(ring_node(0, up))
            greet(ring_node(0, down))
            greet(cross_node(0))
            greet(first_device)
            for col in range(1, NX):
                greet({"ctx": 0, "grp": col})

        @pl.when(wrap_up)
        def _():
            greet(in_next(x))

        @pl.when(wrap_down)
        def _():
            greet(in_prev(x))

    kv_local = []
    bank_local = pltpu.make_async_copy(bank_hbm, col_bank.at[y], local_sem.at[4])
    bank_local.start()
    for j in range(KVH):
        copy = pltpu.make_async_copy(
            kv_hbm.at[:, 0, :, pl.ds(j * HD, HD)],
            kv_buf.at[j, :, pl.ds(0, T), :],
            local_sem.at[j],
        )
        copy.start()
        kv_local.append(copy)
    len_copy = pltpu.make_async_copy(len_hbm, len_buf, local_sem.at[5])
    len_copy.start()
    task_copy = pltpu.make_async_copy(task_hbm, task_buf, local_sem.at[6])
    task_copy.start()
    q_copy = pltpu.make_async_copy(q_hbm.at[0], q_buf, local_sem.at[7])
    q_copy.start()

    def one(flag):
        return jnp.where(flag, 1, 0)

    give_up = (x > 0) & ~last
    take_up = (x > 0) & ~late
    reaches = [x + hop < NX for hop in range(1, NX)]
    spreads = [take_up & (x >= hop) for hop in range(1, NX)]
    from_1, from_2 = x >= 2, x == 3

    partners = 7 + 5 * one(twin) + one(wrap_up | wrap_down)
    pl.semaphore_wait(barrier, jnp.where(zero, 4, partners))

    @pl.when(zero)
    def _():
        for device in ([{"ctx": 0, "grp": col} for col in range(1, NX)] + [twin_device]):
            pl.semaphore_signal(
                ready_sem, inc=1, device_id=device, device_id_type=pl.DeviceIdType.MESH
            )

    def slot_ref(j, slot):
        if slot == 4:
            return pass_buf.at[j]
        return kv_buf.at[j, :, pl.ds(slot * T, T), :]

    sends = []

    def kv_copy(j, number, source, device, target):
        return pltpu.make_async_remote_copy(
            src_ref=slot_ref(j, source),
            dst_ref=slot_ref(j, target),
            send_sem=kv_send.at[number, j],
            recv_sem=kv_recv.at[target - 1, j],
            device_id=device,
            device_id_type=pl.DeviceIdType.MESH,
        )

    def send_kv(flag, j, number, source, device, target):
        @pl.when(flag)
        def _():
            kv_copy(j, number, source, device, target).start()

        sends.append((flag, j, number))

    def wait_kv(flag, j, slot):
        @pl.when(flag)
        def _():
            kv_copy(j, 0, slot, sibling, slot).wait_recv()

    def piece(owner, part, half):
        return col_bank.at[owner, part, pl.ds(HALF * half, HALF)]

    def bank_copy(ref, send_sem, recv_sem, device):
        return pltpu.make_async_remote_copy(
            src_ref=ref,
            dst_ref=ref,
            send_sem=send_sem,
            recv_sem=recv_sem,
            device_id=device,
            device_id_type=pl.DeviceIdType.MESH,
        )

    def ring_copy(half, number, owner, device):
        ref = piece(owner, pair, half)
        return bank_copy(ref, ring_send.at[half, number], ring_recv.at[half, number], device)

    def cross_copy(half, number, owner, part):
        ref = piece(owner, part, half)
        sems = (cross_send.at[half, number], cross_recv.at[half, number])
        return bank_copy(ref, *sems, cross_node(half))

    def sib_copy(turn, number, owner, half):
        ref = piece(owner, pair if turn == 0 else 1 - pair, half)
        return bank_copy(ref, sib_send.at[turn, number], sib_recv.at[turn, number], sibling)

    def down_copy(half, step):
        return ring_copy(half, step, (y + step) % NY, ring_node(half, down))

    def up_copy(half, step):
        return ring_copy(half, 4 + step, (y + NY - step) % NY, ring_node(half, up))

    bank_local.wait()

    @pl.when(live)
    def _():
        down_copy(core, 0).start()

    @pl.when(twin)
    def _():
        down_copy(0, 0).start()

    def give(j):
        send_kv(give_up, j, 3, 0, in_next(x), 4)

    kv_local[0].wait()
    give(0)

    @pl.when(live)
    def _():
        up_copy(core, 0).start()

    @pl.when(twin)
    def _():
        up_copy(0, 0).start()

    for j in range(KVH):
        if j > 0:
            kv_local[j].wait()
        for hop in range(1, NX):
            send_kv(reaches[hop - 1], j, hop - 1, 0, in_row((x + hop) % NX), hop)
    give(1)

    def spread(j):
        wait_kv(take_up, j, 4)
        for hop in (2, 1, 3):
            send_kv(spreads[hop - 1], j, 3 + hop, 4, in_row((x + NX - hop) % NX), NX - hop)

    def ring_step(half, step, share):
        arrivals = [(step, (y + 1 + step) % NY)]
        if step < 3:
            arrivals.append((4 + step, (y + NY - 1 - step) % NY))
        for number, owner in arrivals:
            ring_copy(half, number, owner, sibling).wait_recv()
            if number < 3:
                down_copy(half, step + 1).start()
            if 4 <= number < 6:
                up_copy(half, step + 1).start()
            cross_copy(half, number, owner, pair).start()
            if share:
                sib_copy(0, number, owner, half).start()

    def cross_step(half, step, share):
        arrivals = [(step, (y + 1 + step) % NY)]
        if step < 3:
            arrivals.append((4 + step, (y + NY - 1 - step) % NY))
        for number, owner in arrivals:
            cross_copy(half, number, owner, 1 - pair).wait_recv()
            if share:
                sib_copy(1, number, owner, half).start()

    def on_rings(stage, step):
        @pl.when(~twin)
        def _():
            stage(core, step, True)

        @pl.when(twin)
        def _():
            stage(1, step, False)
            stage(0, step, False)

    ring_owners = [(step, (y + 1 + step) % NY) for step in range(4)]
    ring_owners += [(4 + step, (y + NY - 1 - step) % NY) for step in range(3)]

    def pick_copy(number, slot, device):
        return pltpu.make_async_remote_copy(
            src_ref=pick_out.at[number],
            dst_ref=pick_in.at[slot],
            send_sem=pick_send.at[number],
            recv_sem=pick_recv.at[slot],
            device_id=device,
            device_id_type=pl.DeviceIdType.MESH,
        )

    def pick(ref, place, wants):
        for which in range(2):
            _, owner_y, row = wants[which]
            ref[place, which] = col_bank[owner_y, :, row]

    @pl.when(live)
    def _():
        on_rings(ring_step, 0)

    give(2)

    @pl.when(live)
    def _():
        spread(0)

    len_copy.wait()
    task_copy.wait()
    lengths = len_buf[...]
    starts = scan_lanes(lengths) - lengths
    tasks = task_buf[...]

    def segments(first):
        start_a = jnp.max(jnp.where(starts <= first, starts, 0))
        start_b = jnp.min(jnp.where(starts > first, starts, BIG))
        return start_a, start_b

    def bank_row(start):
        task = jnp.sum(jnp.where(starts == start, tasks, 0))
        row = slot_smem[task]
        owner = (row * 10923) >> 16
        return owner % NX, owner // NX, row - ROWS6 * owner

    slot_a = jnp.where(late & (x == 1), 2, 1)
    slot_b = jnp.where(late & (x == 3), 2, 3)
    slot_late = jnp.where(late & (x == 1), 1, jnp.where(late & (x == 3), 3, 2))

    here_a, here_b = segments(shard * T)
    rel_a = here_a - shard * T
    rel_b = here_b - shard * T

    query_at = lax.broadcasted_iota(jnp.int32, (T, T), 0)
    column = lax.broadcasted_iota(jnp.int32, (T, T), 1)
    earliest = jnp.where(query_at < rel_b, rel_a, rel_b)

    def block_bias(slot):
        key_at = column - slot * T
        return jnp.where((key_at >= earliest) & (key_at <= query_at), 0.0, NEG)

    bias_buf[:, pl.ds(0, T)] = block_bias(0)
    bias_buf[:, pl.ds(T, T)] = block_bias(slot_a)
    bias_buf[:, pl.ds(2 * T, T)] = block_bias(slot_b)
    bias_buf[:, pl.ds(3 * T, T)] = block_bias(slot_late)
    late_bias_buf[:, pl.ds(0, T)] = block_bias(slot_late)
    query_at = lax.broadcasted_iota(jnp.int32, (T, 2 * PREFIX), 0)
    column_p = lax.broadcasted_iota(jnp.int32, (T, 2 * PREFIX), 1)
    late_bias_buf[:, pl.ds(T, 2 * PREFIX)] = jnp.where(
        (query_at < rel_b) == (column_p < PREFIX), 0.0, NEG
    )

    def wanted(first):
        return [bank_row(start) for start in segments(first)]


    @pl.when(live)
    def _():
        on_rings(ring_step, 1)

    give(3)

    @pl.when(live)
    def _():
        on_rings(cross_step, 0)
        spread(1)

    row_wants = [wanted((shard - x + (x + hop) % NX) * T) for hop in range(NX)]

    for slot in (2, 3):

        @pl.when(late & (x < slot))
        def _():
            for j in range(KVH):
                kv_buf[j, :, pl.ds(slot * T, T), :] = jnp.zeros((2, T, HD), jnp.bfloat16)

    @pl.when(live)
    def _():
        on_rings(ring_step, 2)
        on_rings(cross_step, 1)
        spread(2)
        on_rings(ring_step, 3)
        on_rings(cross_step, 2)
        spread(3)
        on_rings(cross_step, 3)

        @pl.when(~twin)
        def _():
            for number, owner in ring_owners:
                for turn in range(2):
                    sib_copy(turn, number, owner, 1 - core).wait_recv()

        for hop in (2, 1, 3):
            col = (x + hop) % NX

            @pl.when(~(late & (col == 0)))
            def _():
                pick(pick_out, hop - 1, row_wants[hop])
                pick_copy(hop - 1, hop, in_row(col)).start()

        pick(pick_in, 0, row_wants[0])

        @pl.when(twin)
        def _():
            for col in range(NX):
                pick(pick_out, NX - 1 + col, wanted(col * T))
            for col in range(1, NX):
                pick_copy(NX - 1 + col, col, {"ctx": 0, "grp": col}).start()
            pl.semaphore_wait(ready_sem, 1)
            pick_copy(NX - 1, 0, first_device).start()

        @pl.when(mate)
        def _():
            pl.semaphore_wait(ready_sem, 1)
            for hop in range(1, NX):

                @pl.when((x + hop) % NX == 0)
                def _():
                    pick(pick_out, hop - 1, row_wants[hop])
                    pick_copy(hop - 1, hop, first_device).start()

    q_copy.wait()

    def row_keys(j, blocks):
        keys = jnp.concatenate(
            [kv_buf[j, 0, pl.ds(pl.multiple_of(s * T, T), T), :] for s in blocks], axis=0
        )
        values = jnp.concatenate(
            [kv_buf[j, 1, pl.ds(pl.multiple_of(s * T, T), T), :] for s in blocks], axis=0
        )
        count = len(blocks) * T
        values = jnp.concatenate([values, jnp.ones((count, HD), jnp.bfloat16)], axis=1)
        for g in range(GROUPS):
            query = q_buf[:, pl.ds(pl.multiple_of((j * GROUPS + g) * HD, HD), HD)]
            scores = lax.dot_general(
                query, keys, (((1,), (1,)), ((), ())), preferred_element_type=jnp.float32
            )
            scores = scores + bias_buf[:, pl.ds(0, count)]
            top = jnp.max(scores, axis=1, keepdims=True)
            weights = jnp.exp2((scores - top) * EXP_SCALE).astype(jnp.bfloat16)
            acc_buf[j, g] = jnp.dot(weights, values, preferred_element_type=jnp.float32)
            max_buf[j, g] = jnp.broadcast_to(top, (T, HD))

    normal = ~late

    @pl.when(normal)
    def _():
        for j in range(KVH):
            for slot in (1, 3, 2):
                wait_kv(normal, j, slot)
            row_keys(j, (0, 1, 3, 2))

    @pl.when(mate)
    def _():
        @pl.loop(0, KVH)
        def _(j):
            wait_kv(from_1, j, 1)
            wait_kv(from_2, j, 2)
            row_keys(j, (0, slot_a, slot_b))

    @pl.when(zero)
    def _():
        @pl.loop(0, KVH)
        def _(j):
            row_keys(j, (0,))

        pick_copy(0, 0, twin_device).wait_recv()

    for hop in range(1, NX):
        pick_copy(0, hop, sibling).wait_recv()
    for which in range(2):
        owner_x, _, _ = row_wants[0][which]
        row = pick_in[(x + NX - owner_x) % NX, which]
        for j in range(KVH):
            for part in range(2):
                kv_buf[j, part, pl.ds(KEYS + which * PREFIX, PREFIX), :] = row[
                    part, :, j * HD : (j + 1) * HD
                ]

    def finish(j, due):
        prefix = pl.ds(KEYS, 2 * PREFIX)
        keys = kv_buf[j, 0, prefix, :]
        values = kv_buf[j, 1, prefix, :]
        bias = late_bias_buf[:, pl.ds(T, 2 * PREFIX)]
        if due:
            block = pl.ds(pl.multiple_of(slot_late * T, T), T)
            keys = jnp.concatenate([kv_buf[j, 0, block, :], keys], axis=0)
            values = jnp.concatenate([kv_buf[j, 1, block, :], values], axis=0)
            bias = late_bias_buf[...]
        count = values.shape[0]
        values = jnp.concatenate([values, jnp.ones((count, HD), jnp.bfloat16)], axis=1)
        for g in range(GROUPS):
            head = pl.ds(pl.multiple_of((j * GROUPS + g) * HD, HD), HD)
            scores = lax.dot_general(
                q_buf[:, head], keys, (((1,), (1,)), ((), ())), preferred_element_type=jnp.float32
            )
            scores = scores + bias
            old_top = max_buf[j, g]
            top = jnp.maximum(old_top, jnp.max(scores, axis=1, keepdims=True))
            shrink = jnp.exp2((old_top - top) * EXP_SCALE)
            tops = top[:, : 2 * PREFIX]
            if due:
                tops = jnp.concatenate([top, tops], axis=1)
            weights = jnp.exp2((scores - tops) * EXP_SCALE).astype(jnp.bfloat16)
            fresh = jnp.dot(weights, values, preferred_element_type=jnp.float32)
            mixed = acc_buf[j, g, :, pl.ds(0, HD)] * shrink + fresh[:, :HD]
            total = acc_buf[j, g, :, pl.ds(HD, HD)] * shrink + fresh[:, HD:]
            out_buf[:, head] = (mixed / total).astype(jnp.bfloat16)
        span = pl.ds(pl.multiple_of(j * GROUPS * HD, GROUPS * HD), GROUPS * HD)
        pltpu.make_async_copy(out_buf.at[:, span], out_hbm.at[0, :, span], out_sem.at[j]).start()

    @pl.when(normal)
    def _():
        for j in range(KVH):
            finish(j, False)

    @pl.when(late)
    def _():
        @pl.loop(0, KVH)
        def _(j):
            @pl.when(mate)
            def _():
                pltpu.make_async_remote_copy(
                    src_ref=kv_buf.at[j, :, pl.ds(0, T), :],
                    dst_ref=kv_buf.at[j, :, pl.ds(slot_late * T, T), :],
                    send_sem=kv_send.at[0, j],
                    recv_sem=kv_recv.at[slot_late - 1, j],
                    device_id=sibling,
                    device_id_type=pl.DeviceIdType.MESH,
                ).wait_recv()

            finish(j, True)

    for flag, j, number in sends:
        keep = flag if number < 4 else flag & live

        @pl.when(keep)
        def _():
            kv_copy(j, number, 0, sibling, 1).wait_send()

    @pl.when(live)
    def _():
        for step in range(4):
            down_copy(core, step).wait_send()
        for step in range(3):
            up_copy(core, step).wait_send()
        for number, owner in ring_owners:
            cross_copy(core, number, owner, pair).wait_send()
        for hop in range(1, NX):
            pick_copy(hop - 1, hop, sibling).wait_send()

        @pl.when(~twin)
        def _():
            for number, owner in ring_owners:
                for turn in range(2):
                    sib_copy(turn, number, owner, core).wait_send()

        @pl.when(twin)
        def _():
            for step in range(4):
                down_copy(0, step).wait_send()
            for step in range(3):
                up_copy(0, step).wait_send()
            for number, owner in ring_owners:
                cross_copy(0, number, owner, pair).wait_send()
            for col in range(NX):
                pick_copy(NX - 1 + col, col, first_device).wait_send()

    for j in range(KVH):
        span = pl.ds(j * GROUPS * HD, GROUPS * HD)
        pltpu.make_async_copy(out_buf.at[:, span], out_hbm.at[0, :, span], out_sem.at[j]).wait()


def on_device(queries, keyvals, seg_len, seg_task, task_slot, prefix_bank):
    anywhere = pl.BlockSpec(memory_space=pl.ANY)
    bf16 = jnp.bfloat16
    return pl.pallas_call(
        kernel,
        out_shape=jax.ShapeDtypeStruct((1, T, H * HD), bf16),
        in_specs=[
            anywhere,
            anywhere,
            anywhere,
            anywhere,
            pl.BlockSpec(memory_space=pltpu.SMEM),
            anywhere,
        ],
        out_specs=anywhere,
        scratch_shapes=[
            pltpu.VMEM((T, H * HD), bf16),
            pltpu.VMEM((KVH, 2, SLOTS, HD), bf16),
            pltpu.VMEM((KVH, 2, T, HD), bf16),
            pltpu.VMEM((NY, 2, ROWS6, PREFIX, KVH * HD), bf16),
            pltpu.VMEM((2 * NX - 1, 2, 2, PREFIX, KVH * HD), bf16),
            pltpu.VMEM((NX, 2, 2, PREFIX, KVH * HD), bf16),
            pltpu.VMEM((KVH, GROUPS, T, 2 * HD), jnp.float32),
            pltpu.VMEM((KVH, GROUPS, T, HD), jnp.float32),
            pltpu.VMEM((T, KEYS), jnp.float32),
            pltpu.VMEM((T, T + 2 * PREFIX), jnp.float32),
            pltpu.VMEM((T, H * HD), bf16),
            pltpu.VMEM((1, SEGS), jnp.int32),
            pltpu.VMEM((1, SEGS), jnp.int32),
            pltpu.SemaphoreType.DMA((8,)),
            pltpu.SemaphoreType.DMA((KVH,)),
            pltpu.SemaphoreType.DMA((7, KVH)),
            pltpu.SemaphoreType.DMA((4, KVH)),
            pltpu.SemaphoreType.DMA((2, 7)),
            pltpu.SemaphoreType.DMA((2, 7)),
            pltpu.SemaphoreType.DMA((2, 7)),
            pltpu.SemaphoreType.DMA((2, 7)),
            pltpu.SemaphoreType.DMA((2, 7)),
            pltpu.SemaphoreType.DMA((2, 7)),
            pltpu.SemaphoreType.DMA((2 * NX - 1,)),
            pltpu.SemaphoreType.DMA((NX,)),
            pltpu.SemaphoreType.REGULAR,
        ],
        compiler_params=pltpu.CompilerParams(
            collective_id=0, has_side_effects=True, vmem_limit_bytes=67043328
        ),
    )(queries, keyvals, seg_len, seg_task, task_slot, prefix_bank)


def solution(mesh):
    in_specs = (
        P(None, ("ctx", "grp"), None),
        P(None, None, ("ctx", "grp"), None),
        P(),
        P(),
        P(),
        P(None, "grp", None, None),
    )
    out_specs = P(None, ("ctx", "grp"), None)
    return jax.shard_map(
        on_device, mesh=mesh, in_specs=in_specs, out_specs=out_specs, check_vma=False
    )
```

```python
import math

import jax
import jax.numpy as jnp
from jax import lax
from jax.experimental import pallas as pl
from jax.experimental.pallas import tpu as pltpu
from jax.sharding import PartitionSpec as P

H = 32
KVH = 4
HD = 128
GROUPS = H // KVH
T = 128
PREFIX = 16
SEGS = 512
ROWS6 = 6
NX = 4
NY = 8
KEYS = 4 * T
SLOTS = KEYS + 2 * PREFIX
EXP_SCALE = math.log2(math.e) / math.sqrt(HD)
NEG = -1e30
BIG = 1 << 30


def scan_lanes(row):
    lane = lax.broadcasted_iota(jnp.int32, row.shape, 1)
    step = 1
    while step < row.shape[1]:
        row = row + jnp.where(lane >= step, pltpu.roll(row, step, 1), 0)
        step *= 2
    return row


def kernel(
    q_hbm,
    kv_hbm,
    len_hbm,
    task_hbm,
    slot_smem,
    bank_hbm,
    out_hbm,
    q_buf,
    kv_buf,
    pass_buf,
    col_bank,
    pick_out,
    pick_in,
    acc_buf,
    max_buf,
    bias_buf,
    late_bias_buf,
    out_buf,
    len_buf,
    task_buf,
    local_sem,
    out_sem,
    kv_send,
    kv_recv,
    ring_send,
    ring_recv,
    pick_send,
    pick_recv,
    ready_sem,
):
    ctx = lax.axis_index("ctx")
    grp = lax.axis_index("grp")
    n_ctx = lax.axis_size("ctx")
    core = ctx % 2
    x = grp % NX
    y = grp // NX
    shard = ctx * (NX * NY) + grp

    zero = shard == 0
    live = shard != 0
    twin = (ctx == 1) & (grp == 0)
    late = (ctx == 0) & (y == 0)
    mate = late & (x > 0)
    last = (ctx == n_ctx - 1) & (y == NY - 1)

    next_ctx = jnp.where(y == NY - 1, (ctx + 1) % n_ctx, ctx)
    prev_ctx = jnp.where(y == 0, (ctx + n_ctx - 1) % n_ctx, ctx)
    other = ctx + 1 - 2 * core
    pair_ctx = (ctx, other)
    first_chips = (ctx < 2) & (y == 0)
    up = (y + 1) % NY
    down = (y + NY - 1) % NY

    def in_row(col):
        return {"ctx": ctx, "grp": y * NX + col}

    def in_next(col):
        return {"ctx": next_ctx, "grp": up * NX + col}

    def in_prev(col):
        return {"ctx": prev_ctx, "grp": down * NX + col}

    def ring_node(half, row):
        skip = (ctx < 2) & (x == 0) & (row == 0)
        return {"ctx": jnp.where(skip, 1, ctx - core + half), "grp": row * NX + x}

    sibling = {"ctx": ctx + 1 - 2 * core, "grp": grp}
    first_device = {"ctx": 0, "grp": 0}
    twin_device = {"ctx": 1, "grp": 0}

    barrier = pltpu.get_barrier_semaphore()

    def greet(device):
        pl.semaphore_signal(barrier, inc=1, device_id=device, device_id_type=pl.DeviceIdType.MESH)

    wrap_up = (x > 0) & (y == NY - 1) & ~last
    wrap_down = (x > 0) & (y == 0) & ~late

    @pl.when(live)
    def _():
        for hop in range(1, NX):
            col = (x + hop) % NX
            for target in pair_ctx:

                @pl.when(~(first_chips & (target == 0) & (col == 0)))
                def _():
                    greet({"ctx": target, "grp": y * NX + col})

        greet(ring_node(core, up))
        greet(ring_node(core, down))

        @pl.when(~twin)
        def _():
            greet(sibling)

        @pl.when(first_chips)
        def _():
            greet(first_device)

        @pl.when(twin)
        def _():
            greet(ring_node(0, up))
            greet(ring_node(0, down))

        @pl.when(wrap_up)
        def _():
            greet(in_next(x))

        @pl.when(wrap_down)
        def _():
            greet(in_prev(x))

    kv_local = []
    bank_local = pltpu.make_async_copy(bank_hbm, col_bank.at[y], local_sem.at[4])
    bank_local.start()
    for j in range(KVH):
        copy = pltpu.make_async_copy(
            kv_hbm.at[:, 0, :, pl.ds(j * HD, HD)],
            kv_buf.at[j, :, pl.ds(0, T), :],
            local_sem.at[j],
        )
        copy.start()
        kv_local.append(copy)
    len_copy = pltpu.make_async_copy(len_hbm, len_buf, local_sem.at[5])
    len_copy.start()
    task_copy = pltpu.make_async_copy(task_hbm, task_buf, local_sem.at[6])
    task_copy.start()
    q_copy = pltpu.make_async_copy(q_hbm.at[0], q_buf, local_sem.at[7])
    q_copy.start()

    def one(flag):
        return jnp.where(flag, 1, 0)

    give_up = (x > 0) & ~last
    take_up = (x > 0) & ~late
    reaches = [x + hop < NX for hop in range(1, NX)]
    spreads = [take_up & (x >= hop) for hop in range(1, NX)]
    from_1, from_2 = x >= 2, x == 3

    partners = 9 - one(first_chips) + 2 * one(twin) + one(wrap_up | wrap_down)
    pl.semaphore_wait(barrier, jnp.where(zero, 7, partners))

    @pl.when(zero)
    def _():
        devices = [{"ctx": c, "grp": col} for c in range(2) for col in range(NX) if c + col]
        for device in devices:
            pl.semaphore_signal(
                ready_sem, inc=1, device_id=device, device_id_type=pl.DeviceIdType.MESH
            )

    def slot_ref(j, slot):
        if slot == 4:
            return pass_buf.at[j]
        return kv_buf.at[j, :, pl.ds(slot * T, T), :]

    sends = []

    def kv_copy(j, number, source, device, target):
        return pltpu.make_async_remote_copy(
            src_ref=slot_ref(j, source),
            dst_ref=slot_ref(j, target),
            send_sem=kv_send.at[number, j],
            recv_sem=kv_recv.at[target - 1, j],
            device_id=device,
            device_id_type=pl.DeviceIdType.MESH,
        )

    def send_kv(flag, j, number, source, device, target):
        @pl.when(flag)
        def _():
            kv_copy(j, number, source, device, target).start()

        sends.append((flag, j, number))

    def wait_kv(flag, j, slot):
        @pl.when(flag)
        def _():
            kv_copy(j, 0, slot, sibling, slot).wait_recv()

    def ring_copy(part, number, third, owner, device):
        piece = col_bank.at[owner, part, pl.ds(2 * third, 2)]
        return pltpu.make_async_remote_copy(
            src_ref=piece,
            dst_ref=piece,
            send_sem=ring_send.at[part, number, third],
            recv_sem=ring_recv.at[part, number, third],
            device_id=device,
            device_id_type=pl.DeviceIdType.MESH,
        )

    def down_copy(part, step, third):
        return ring_copy(part, step, third, (y + step) % NY, ring_node(part, down))

    def up_copy(part, step, third):
        return ring_copy(part, 4 + step, third, (y + NY - step) % NY, ring_node(part, up))

    def first_pieces(part, send):
        for third in range(3):
            send(part, 0, third).start()

    bank_local.wait()

    @pl.when(live)
    def _():
        first_pieces(core, down_copy)

    @pl.when(twin)
    def _():
        first_pieces(0, down_copy)

    def give(j):
        send_kv(give_up, j, 3, 0, in_next(x), 4)

    kv_local[0].wait()
    give(0)

    @pl.when(live)
    def _():
        first_pieces(core, up_copy)

    @pl.when(twin)
    def _():
        first_pieces(0, up_copy)

    for j in range(KVH):
        if j > 0:
            kv_local[j].wait()
        for hop in range(1, NX):
            send_kv(reaches[hop - 1], j, hop - 1, 0, in_row((x + hop) % NX), hop)
    give(1)

    def spread(j):
        wait_kv(take_up, j, 4)
        for hop in (2, 1, 3):
            send_kv(spreads[hop - 1], j, 3 + hop, 4, in_row((x + NX - hop) % NX), NX - hop)

    def ring_step(part, step):
        for third in range(3):
            owner = (y + 1 + step) % NY
            ring_copy(part, step, third, owner, sibling).wait_recv()
            if step < 3:
                down_copy(part, step + 1, third).start()
                owner = (y + NY - 1 - step) % NY
                ring_copy(part, 4 + step, third, owner, sibling).wait_recv()
            if step < 2:
                up_copy(part, step + 1, third).start()

    def rings(step):
        ring_step(core, step)

        @pl.when(twin)
        def _():
            ring_step(0, step)

    def pick(ref, part, wants):
        for which in range(2):
            _, owner_y, row = wants[which]
            ref[which] = col_bank[owner_y, part, row]

    def pick_copy(group, part, pair, hop, device):
        return pltpu.make_async_remote_copy(
            src_ref=pick_out.at[group, pair, hop],
            dst_ref=pick_in.at[part, hop],
            send_sem=pick_send.at[group, pair, hop],
            recv_sem=pick_recv.at[part, hop],
            device_id=device,
            device_id_type=pl.DeviceIdType.MESH,
        )

    def send_pick(group, part, pair, hop):
        device = {"ctx": pair_ctx[pair], "grp": y * NX + (x + hop) % NX}
        pick(pick_out.at[group, pair, hop], part, row_wants[pair][hop])
        pick_copy(group, part, pair, hop, device).start()

    @pl.when(live)
    def _():
        rings(0)

    give(2)

    @pl.when(live)
    def _():
        spread(0)

    len_copy.wait()
    task_copy.wait()
    lengths = len_buf[...]
    starts = scan_lanes(lengths) - lengths
    tasks = task_buf[...]

    def segments(first):
        start_a = jnp.max(jnp.where(starts <= first, starts, 0))
        start_b = jnp.min(jnp.where(starts > first, starts, BIG))
        return start_a, start_b

    def bank_row(start):
        task = jnp.sum(jnp.where(starts == start, tasks, 0))
        row = slot_smem[task]
        owner = (row * 10923) >> 16
        return owner % NX, owner // NX, row - ROWS6 * owner

    slot_a = jnp.where(late & (x == 1), 2, 1)
    slot_b = jnp.where(late & (x == 3), 2, 3)
    slot_late = jnp.where(late & (x == 1), 1, jnp.where(late & (x == 3), 3, 2))

    here_a, here_b = segments(shard * T)
    rel_a = here_a - shard * T
    rel_b = here_b - shard * T

    query_at = lax.broadcasted_iota(jnp.int32, (T, T), 0)
    column = lax.broadcasted_iota(jnp.int32, (T, T), 1)
    earliest = jnp.where(query_at < rel_b, rel_a, rel_b)

    def block_bias(slot):
        key_at = column - slot * T
        return jnp.where((key_at >= earliest) & (key_at <= query_at), 0.0, NEG)

    bias_buf[:, pl.ds(0, T)] = block_bias(0)
    bias_buf[:, pl.ds(T, T)] = block_bias(slot_a)
    bias_buf[:, pl.ds(2 * T, T)] = block_bias(slot_b)
    bias_buf[:, pl.ds(3 * T, T)] = block_bias(slot_late)
    late_bias_buf[:, pl.ds(0, T)] = block_bias(slot_late)
    query_at = lax.broadcasted_iota(jnp.int32, (T, 2 * PREFIX), 0)
    column_p = lax.broadcasted_iota(jnp.int32, (T, 2 * PREFIX), 1)
    late_bias_buf[:, pl.ds(T, 2 * PREFIX)] = jnp.where(
        (query_at < rel_b) == (column_p < PREFIX), 0.0, NEG
    )

    def wanted(first):
        return [bank_row(start) for start in segments(first)]


    @pl.when(live)
    def _():
        rings(1)

    give(3)

    @pl.when(live)
    def _():
        spread(1)

    row_wants = [
        [wanted((c * NX * NY + y * NX + (x + hop) % NX) * T) for hop in range(NX)]
        for c in pair_ctx
    ]

    for slot in (2, 3):

        @pl.when(late & (x < slot))
        def _():
            for j in range(KVH):
                kv_buf[j, :, pl.ds(slot * T, T), :] = jnp.zeros((2, T, HD), jnp.bfloat16)

    @pl.when(live)
    def _():
        rings(2)
        spread(2)
        rings(3)
        spread(3)

        for hop in (2, 1, 3):
            for pair in range(2):
                from_first = first_chips & (pair_ctx[pair] == 0) & ((x + hop) % NX == 0)

                @pl.when(~from_first)
                def _():
                    send_pick(0, core, pair, hop)

        @pl.when(~twin)
        def _():
            send_pick(0, core, 1, 0)

        pick(pick_in.at[core, 0], core, row_wants[0][0])

        @pl.when(twin)
        def _():
            for hop in (2, 1, 3):
                for pair in range(2):
                    send_pick(1, 0, pair, hop)
            pick(pick_in.at[0, 0], 0, row_wants[0][0])

        @pl.when(first_chips)
        def _():
            pl.semaphore_wait(ready_sem, 1)
            for hop in range(NX):
                for pair in range(2):
                    if pair + hop:
                        to_first = (pair_ctx[pair] == 0) & ((x + hop) % NX == 0)

                        @pl.when(to_first)
                        def _():
                            send_pick(0, core, pair, hop)

            @pl.when(twin)
            def _():
                send_pick(1, 0, 1, 0)

    q_copy.wait()

    def row_keys(j, blocks):
        keys = jnp.concatenate(
            [kv_buf[j, 0, pl.ds(pl.multiple_of(s * T, T), T), :] for s in blocks], axis=0
        )
        values = jnp.concatenate(
            [kv_buf[j, 1, pl.ds(pl.multiple_of(s * T, T), T), :] for s in blocks], axis=0
        )
        count = len(blocks) * T
        values = jnp.concatenate([values, jnp.ones((count, HD), jnp.bfloat16)], axis=1)
        for g in range(GROUPS):
            query = q_buf[:, pl.ds(pl.multiple_of((j * GROUPS + g) * HD, HD), HD)]
            scores = lax.dot_general(
                query, keys, (((1,), (1,)), ((), ())), preferred_element_type=jnp.float32
            )
            scores = scores + bias_buf[:, pl.ds(0, count)]
            top = jnp.max(scores, axis=1, keepdims=True)
            weights = jnp.exp2((scores - top) * EXP_SCALE).astype(jnp.bfloat16)
            acc_buf[j, g] = jnp.dot(weights, values, preferred_element_type=jnp.float32)
            max_buf[j, g] = jnp.broadcast_to(top, (T, HD))

    normal = ~late

    @pl.when(normal)
    def _():
        for j in range(KVH):
            for slot in (1, 3, 2):
                wait_kv(normal, j, slot)
            row_keys(j, (0, 1, 3, 2))

    @pl.when(mate)
    def _():
        @pl.loop(0, KVH)
        def _(j):
            wait_kv(from_1, j, 1)
            wait_kv(from_2, j, 2)
            row_keys(j, (0, slot_a, slot_b))

    @pl.when(zero)
    def _():
        @pl.loop(0, KVH)
        def _(j):
            row_keys(j, (0,))

        pick_copy(0, 0, 0, 0, twin_device).wait_recv()

    @pl.when(~twin)
    def _():
        pick_copy(0, 1 - core, 0, 0, sibling).wait_recv()

    for part in range(2):
        for hop in range(1, NX):
            pick_copy(0, part, 0, hop, sibling).wait_recv()
    for which in range(2):
        owner_x, _, _ = row_wants[0][0][which]
        for part in range(2):
            row = pick_in[part, (x + NX - owner_x) % NX, which]
            for j in range(KVH):
                kv_buf[j, part, pl.ds(KEYS + which * PREFIX, PREFIX), :] = row[
                    :, j * HD : (j + 1) * HD
                ]

    def finish(j, due):
        prefix = pl.ds(KEYS, 2 * PREFIX)
        keys = kv_buf[j, 0, prefix, :]
        values = kv_buf[j, 1, prefix, :]
        bias = late_bias_buf[:, pl.ds(T, 2 * PREFIX)]
        if due:
            block = pl.ds(pl.multiple_of(slot_late * T, T), T)
            keys = jnp.concatenate([kv_buf[j, 0, block, :], keys], axis=0)
            values = jnp.concatenate([kv_buf[j, 1, block, :], values], axis=0)
            bias = late_bias_buf[...]
        count = values.shape[0]
        values = jnp.concatenate([values, jnp.ones((count, HD), jnp.bfloat16)], axis=1)
        for g in range(GROUPS):
            head = pl.ds(pl.multiple_of((j * GROUPS + g) * HD, HD), HD)
            scores = lax.dot_general(
                q_buf[:, head], keys, (((1,), (1,)), ((), ())), preferred_element_type=jnp.float32
            )
            scores = scores + bias
            old_top = max_buf[j, g]
            top = jnp.maximum(old_top, jnp.max(scores, axis=1, keepdims=True))
            shrink = jnp.exp2((old_top - top) * EXP_SCALE)
            tops = top[:, : 2 * PREFIX]
            if due:
                tops = jnp.concatenate([top, tops], axis=1)
            weights = jnp.exp2((scores - tops) * EXP_SCALE).astype(jnp.bfloat16)
            fresh = jnp.dot(weights, values, preferred_element_type=jnp.float32)
            mixed = acc_buf[j, g, :, pl.ds(0, HD)] * shrink + fresh[:, :HD]
            total = acc_buf[j, g, :, pl.ds(HD, HD)] * shrink + fresh[:, HD:]
            out_buf[:, head] = (mixed / total).astype(jnp.bfloat16)
        span = pl.ds(pl.multiple_of(j * GROUPS * HD, GROUPS * HD), GROUPS * HD)
        pltpu.make_async_copy(out_buf.at[:, span], out_hbm.at[0, :, span], out_sem.at[j]).start()

    @pl.when(normal)
    def _():
        for j in range(KVH):
            finish(j, False)

    @pl.when(late)
    def _():
        @pl.loop(0, KVH)
        def _(j):
            @pl.when(mate)
            def _():
                pltpu.make_async_remote_copy(
                    src_ref=kv_buf.at[j, :, pl.ds(0, T), :],
                    dst_ref=kv_buf.at[j, :, pl.ds(slot_late * T, T), :],
                    send_sem=kv_send.at[0, j],
                    recv_sem=kv_recv.at[slot_late - 1, j],
                    device_id=sibling,
                    device_id_type=pl.DeviceIdType.MESH,
                ).wait_recv()

            finish(j, True)

    for flag, j, number in sends:
        keep = flag if number < 4 else flag & live

        @pl.when(keep)
        def _():
            kv_copy(j, number, 0, sibling, 1).wait_send()

    @pl.when(live)
    def _():
        for third in range(3):
            for step in range(4):
                down_copy(core, step, third).wait_send()
            for step in range(3):
                up_copy(core, step, third).wait_send()
        for pair in range(2):
            for hop in range(NX):
                if pair + hop:
                    pick_copy(0, core, pair, hop, sibling).wait_send()

        @pl.when(twin)
        def _():
            for third in range(3):
                for step in range(4):
                    down_copy(0, step, third).wait_send()
                for step in range(3):
                    up_copy(0, step, third).wait_send()
            for pair in range(2):
                for hop in range(NX):
                    if pair + hop:
                        pick_copy(1, 0, pair, hop, sibling).wait_send()

    for j in range(KVH):
        span = pl.ds(j * GROUPS * HD, GROUPS * HD)
        pltpu.make_async_copy(out_buf.at[:, span], out_hbm.at[0, :, span], out_sem.at[j]).wait()


def on_device(queries, keyvals, seg_len, seg_task, task_slot, prefix_bank):
    anywhere = pl.BlockSpec(memory_space=pl.ANY)
    bf16 = jnp.bfloat16
    return pl.pallas_call(
        kernel,
        out_shape=jax.ShapeDtypeStruct((1, T, H * HD), bf16),
        in_specs=[
            anywhere,
            anywhere,
            anywhere,
            anywhere,
            pl.BlockSpec(memory_space=pltpu.SMEM),
            anywhere,
        ],
        out_specs=anywhere,
        scratch_shapes=[
            pltpu.VMEM((T, H * HD), bf16),
            pltpu.VMEM((KVH, 2, SLOTS, HD), bf16),
            pltpu.VMEM((KVH, 2, T, HD), bf16),
            pltpu.VMEM((NY, 2, ROWS6, PREFIX, KVH * HD), bf16),
            pltpu.VMEM((2, 2, NX, 2, PREFIX, KVH * HD), bf16),
            pltpu.VMEM((2, NX, 2, PREFIX, KVH * HD), bf16),
            pltpu.VMEM((KVH, GROUPS, T, 2 * HD), jnp.float32),
            pltpu.VMEM((KVH, GROUPS, T, HD), jnp.float32),
            pltpu.VMEM((T, KEYS), jnp.float32),
            pltpu.VMEM((T, T + 2 * PREFIX), jnp.float32),
            pltpu.VMEM((T, H * HD), bf16),
            pltpu.VMEM((1, SEGS), jnp.int32),
            pltpu.VMEM((1, SEGS), jnp.int32),
            pltpu.SemaphoreType.DMA((8,)),
            pltpu.SemaphoreType.DMA((KVH,)),
            pltpu.SemaphoreType.DMA((7, KVH)),
            pltpu.SemaphoreType.DMA((4, KVH)),
            pltpu.SemaphoreType.DMA((2, 7, 3)),
            pltpu.SemaphoreType.DMA((2, 7, 3)),
            pltpu.SemaphoreType.DMA((2, 2, NX)),
            pltpu.SemaphoreType.DMA((2, NX)),
            pltpu.SemaphoreType.REGULAR,
        ],
        compiler_params=pltpu.CompilerParams(
            collective_id=0, has_side_effects=True, vmem_limit_bytes=67043328
        ),
    )(queries, keyvals, seg_len, seg_task, task_slot, prefix_bank)


def solution(mesh):
    in_specs = (
        P(None, ("ctx", "grp"), None),
        P(None, None, ("ctx", "grp"), None),
        P(),
        P(),
        P(),
        P(None, "grp", None, None),
    )
    out_specs = P(None, ("ctx", "grp"), None)
    return jax.shard_map(
        on_device, mesh=mesh, in_specs=in_specs, out_specs=out_specs, check_vma=False
    )
```
